32 devices in a mesh: grp: 2 (over y), cin: 4 (over z), cout: 4 (over x, core).
Axes of the slice: x: 2, y: 2, z: 4, core: 2. Of those that a mesh axis runs over, the one named last changes fastest.
Arguments:
- volume: bfloat16 [128, 8, 16, 256], P(None, ('grp', 'cin'), 'cout'), parts along dimension 1, may hold values from -6 to 6
- first_filter: bfloat16 [128, 27, 128], replicated, may hold values from -0.109375 to 0.109375
- second_filter: bfloat16 [128, 27, 128], replicated, may hold values from -0.109375 to 0.109375
- cotangent: bfloat16 [128, 8, 16, 256], P(None, ('grp', 'cin'), 'cout'), parts along dimension 1, may hold values from -6 to 6
Outputs:
- second_out: bfloat16 [128, 8, 16, 256], P(None, ('grp', 'cin'), 'cout'), parts along dimension 1
- first_filter_grad: float32 [128, 54, 128], P('cout', 'grp', 'cin'), parts along dimension 1
- second_filter_grad: float32 [128, 54, 128], P('cout', 'grp', 'cin'), parts along dimension 1
The draws below stay inside these ranges and needn't reach their ends.
There are 2 independent parts, one for each index of `grp`. The reference program is written for one: setup_inputs(seed, part) draws one part's arguments, and reference() takes and returns one part's arrays. A program takes and returns all parts, laid end to end along the dimension named above; an argument that names none is the same for every part. Nothing has to cross between parts.
All inputs are finite; a program needn't handle non-finite values.
Results may differ from the reference program's by a relative error of at most 0.005.
Values may be sent and summed in bfloat16 or wider, within the bound.
No kernel may reach another device: no remote copies, remote signals or barrier semaphores. Data moves between devices by JAX's collectives and lax.ppermute only.
A program may use at most 64 MiB of HBM per device.

```python
import math
import jax
import jax.numpy as jnp
from jax import lax

C = 128
X = 256
P_SIZE = 4
Y = 16


def steps_of(stream_key, extent, shards, smallest, largest):
    def one(dim, blocks):
        heights = jax.random.uniform(jax.random.fold_in(jax.random.fold_in(stream_key, 6), dim), (blocks,), jnp.float32, smallest / len(shards), largest / len(shards))
        return jnp.repeat(jnp.exp(heights), extent[dim] // blocks).reshape((-1,) + (1,) * (len(extent) - dim - 1))

    gain = one(*shards[0])
    for cut in shards[1:]:
        gain = gain * one(*cut)
    return gain


def noise(key, extent, scale, bound, shards=(), held_as=jnp.bfloat16):
    level = steps_of(key, extent, shards, -0.22, 0.18) if shards else 1.0
    array = jax.random.normal(key, extent, jnp.float32) * scale * level
    return jnp.minimum(jnp.maximum(array, -bound), bound).astype(held_as)


def setup_inputs(seed: int = 0, part: int = 0) -> dict:
    key_of = jax.random.split(jax.random.key(seed), 5)
    part_splits = jax.random.split(jax.random.fold_in(key_of[4], part), 5)
    volume = noise(part_splits[0], (C, P_SIZE, Y, X), 1.0, 6.0, ((1, 4), (2, 4)))
    first_filter = noise(key_of[1], (C, 27, C), (27 * C) ** -0.5, 0.109375)
    second_filter = noise(key_of[2], (C, 27, C), (27 * C) ** -0.5, 0.109375)
    cotangent = noise(part_splits[3], (C, P_SIZE, Y, X), 1.0, 6.0, ((1, 4), (2, 4)))
    return {"volume": volume, "first_filter": first_filter, "second_filter": second_filter, "cotangent": cotangent}


def conv_same(field, weight):
    outs = weight.shape[0]
    ins = weight.shape[2]
    kernel = weight.reshape(outs, 3, 3, 3, ins).transpose(0, 4, 1, 2, 3)
    result = lax.conv_general_dilated(field[None], kernel, (1, 1, 1), ((1, 1), (1, 1), (1, 1)), dimension_numbers=('NCDHW', 'OIDHW', 'NCDHW'), precision=lax.Precision.HIGHEST)
    return result[0]

def reference(volume, first_filter, second_filter, cotangent):
    factor = 1.0 / math.sqrt(P_SIZE * Y * X)
    volume_wide = volume.astype(jnp.float32)
    first_wide = first_filter.astype(jnp.float32)
    second_wide = second_filter.astype(jnp.float32)
    first_out = conv_same(volume_wide, first_wide)
    hidden = jax.nn.silu(first_out).astype(jnp.bfloat16)
    second_raw, second_pull = jax.vjp(conv_same, hidden.astype(jnp.float32), second_wide)
    second_out = second_raw.astype(jnp.bfloat16)
    hidden_grad, second_raw_grad = second_pull(cotangent.astype(jnp.float32))
    logistic = jax.nn.sigmoid(first_out)
    first_grad = (hidden_grad * logistic * (1.0 + first_out * (1.0 - logistic))).astype(jnp.bfloat16)
    unused, first_pull = jax.vjp(lambda weight: conv_same(volume_wide, weight), first_wide)
    first_raw_grad = first_pull(first_grad.astype(jnp.float32))[0]
    return (second_out, first_raw_grad * factor, second_raw_grad * factor)
```

```python
import functools
import math

import jax
import jax.numpy as jnp
from jax import lax
from jax.experimental import pallas as pl
from jax.experimental.pallas import tpu as pltpu
from jax.sharding import PartitionSpec as P

VMEM = pl.BlockSpec(memory_space=pltpu.VMEM)
SMEM = pl.BlockSpec(memory_space=pltpu.SMEM)
ANY = pl.BlockSpec(memory_space=pl.ANY)
F32 = jnp.float32
BF16 = jnp.bfloat16


def links(count, odd):
    pairs = []
    for i in range(odd, count - 1, 2):
        pairs += [(i, i + 1), (i + 1, i)]
    return pairs


def swap_planes(values, odd):
    return lax.ppermute(values, "cin", links(lax.axis_size("cin"), odd))


def swap_rows(values, odd):
    return lax.ppermute(values, "cout", links(lax.axis_size("cout"), odd))


def swap_corner(values, odd):
    count = lax.axis_size("cout")
    pairs = [
        (a * count + c, b * count + d)
        for a, b in links(lax.axis_size("cin"), odd)
        for c, d in links(count, 1)
    ]
    return lax.ppermute(values, ("cin", "cout"), pairs)


def shift_up(values):
    lane = lax.broadcasted_iota(jnp.int32, values.shape, 1)
    return jnp.where(lane == 0, 0.0, pltpu.roll(values, 1, 1))


def shift_down(values):
    width = values.shape[1]
    lane = lax.broadcasted_iota(jnp.int32, values.shape, 1)
    return jnp.where(lane == width - 1, 0.0, pltpu.roll(values, width - 1, 1))


def spread(values):
    wide = values.astype(F32)
    return jnp.concatenate(
        [shift_down(wide).astype(BF16), values.astype(BF16), shift_up(wide).astype(BF16)], axis=0
    )


def combine(products):
    chans = products.shape[0] // 3
    return (
        products[chans : 2 * chans]
        + shift_up(products[:chans])
        + shift_down(products[2 * chans :])
    )


def fill(where, slabs, field, sems):
    rows = slabs[0].shape[0]
    plane = where[0]
    row = where[1]
    even_plane = 2 * (1 - plane)
    odd_plane = 2 * plane
    body = pl.ds(1, rows)
    even_row = (1 - row) * (rows + 1)
    odd_row = row * (rows + 1)
    source = row * (rows - 1)
    targets = (1, even_plane, odd_plane)
    copies = []
    for k in range(3):
        copies.append((slabs[k], field.at[body, targets[k]]))
        copies.append((slabs[3 + k].at[source], field.at[even_row, targets[k]]))
        copies.append((slabs[6 + k], field.at[odd_row, targets[k]]))
    started = [
        pltpu.make_async_copy(src, dst, sems.at[n]) for n, (src, dst) in enumerate(copies)
    ]
    for copy in started:
        copy.start()
    for copy in started:
        copy.wait()


def window(field, row):
    block = field[pl.ds(row, 3)]
    return block.reshape(-1, block.shape[-1])


def conv_rows(weights, field, row):
    return combine(
        jnp.dot(weights[...], window(field, row), preferred_element_type=F32)
    )


def first_kernel(where, *refs):
    slabs = refs[:9]
    weights, field, hidden, slope, edge, sems = refs[9:]
    fill(where, slabs, field, sems)
    rows = hidden.shape[0]

    def step(row, carry):
        value = conv_rows(weights, field, row)
        gate = 1.0 / (1.0 + jnp.exp(-value))
        hidden[row] = (value * gate).astype(BF16)
        slope[row] = gate * (1.0 + value * (1.0 - gate))
        return carry

    lax.fori_loop(0, rows, step, 0)
    edge[...] = hidden[where[1] * (rows - 1)]


def second_kernel(where, *refs):
    slabs = refs[:9]
    weights, out, field, sems = refs[9:]
    fill(where, slabs, field, sems)

    def step(row, carry):
        out[row] = conv_rows(weights, field, row).astype(BF16)
        return carry

    lax.fori_loop(0, out.shape[0], step, 0)


def hand_over(where, total, *outs):
    if len(outs) == 1:
        outs[0][...] = total[...]
        return
    send, keep = outs
    width = send.shape[1] // 2
    mine = where[1]
    for half in range(2):
        rows = pl.ds(half * width, width)
        theirs = pl.multiple_of(2 * half * width + (1 - mine) * width, width)
        ours = pl.multiple_of(2 * half * width + mine * width, width)
        send[:, rows] = total[:, pl.ds(theirs, width)].astype(BF16)
        keep[:, rows] = total[:, pl.ds(ours, width)]


def second_grad_kernel(where, *refs):
    slabs = refs[:9]
    hidden, field, *outs = refs[9:-2]
    total, sems = refs[-2:]
    fill(where, slabs, field, sems)
    taps, chans, width = total.shape

    def step(row, carry):
        part = lax.dot_general(
            window(field, row),
            spread(hidden[row]),
            (((1,), (1,)), ((), ())),
            preferred_element_type=F32,
        ).reshape(taps, chans, width)
        total[...] = jnp.where(row == 0, part, total[...] + part)
        return carry

    lax.fori_loop(0, hidden.shape[0], step, 0)
    hand_over(where, total, *outs)


def first_grad_kernel(where, weights, grad_field, slope, field, *refs):
    outs = refs[:-1]
    total = refs[-1]
    taps, chans, width = total.shape

    def step(row, carry):
        grad = conv_rows(weights, grad_field, row) * slope[row]
        part = lax.dot_general(
            spread(grad.astype(BF16)),
            window(field, row),
            (((1,), (1,)), ((), ())),
            preferred_element_type=F32,
        ).reshape(taps, chans, width)
        total[...] = jnp.where(row == 0, part, total[...] + part)
        return carry

    lax.fori_loop(0, slope.shape[0], step, 0)
    hand_over(where, total, *outs)


def add_kernel(where, held, arrived, send, keep):
    width = send.shape[1]
    mine = where[2]
    ours = pl.ds(pl.multiple_of(mine * width, width), width)
    theirs = pl.ds(pl.multiple_of((1 - mine) * width, width), width)
    send[...] = (held[:, theirs] + arrived[:, theirs].astype(F32)).astype(BF16)
    keep[...] = held[:, ours] + arrived[:, ours].astype(F32)


def pack_kernel(where, held, arrived, *refs):
    sends = refs[:-2]
    keep, packed = refs[-2:]
    parts, tiles, outs, lanes = packed.shape
    group = lanes // parts
    per = held.shape[2] // lanes
    sums = {}
    for n in range(held.shape[0] * per):
        at = (n // per, slice(None), slice(n % per * lanes, (n % per + 1) * lanes))
        sums[n] = held[at] + arrived[at].astype(F32)
    lane = lax.broadcasted_iota(jnp.int32, (outs, lanes), 1) // group
    for tile in range(tiles):
        for part in range(parts):
            value = jnp.zeros((outs, lanes), F32)
            for place in range(parts):
                n = tile * parts + place
                if n in sums:
                    turned = sums[n]
                    if place != part:
                        turned = pltpu.roll(turned, (place - part) % parts * group, 1)
                    value = jnp.where(lane == place, turned, value)
            packed[part, tile] = value
    mine = where[3]
    keep[...] = packed[mine]
    for k, send in enumerate(sends):
        send[...] = packed[mine ^ (k + 1)].astype(BF16)


def finish_kernel(tap_of, factor, held, *refs):
    out = refs[-1]
    tiles, outs, lanes = held.shape
    group = out.shape[2]
    places = lanes // group
    for tile in range(tiles):
        total = held[tile]
        for arrived in refs[:-1]:
            total = total + arrived[tile].astype(F32)
        total = total * factor
        for place in range(places):
            n = tile * places + place
            if n < len(tap_of):
                out[:, tap_of[n], :] = total[:, place * group : (place + 1) * group]


def struct(shape, dtype):
    return jax.ShapeDtypeStruct(shape, dtype)


def call(kernel, name, ins, out_shapes, args, scratch=(), flops=0):
    moved = sum(math.prod(a.shape) * a.dtype.itemsize for a in (*args, *out_shapes))
    return pl.pallas_call(
        kernel,
        name=name,
        in_specs=ins,
        out_specs=[VMEM] * len(out_shapes),
        out_shape=out_shapes,
        scratch_shapes=scratch,
        cost_estimate=pl.CostEstimate(flops=flops, bytes_accessed=moved, transcendentals=0),
    )(*args)


def slabs_of(own, edge_own, edge_even, edge_odd):
    planes = (own, swap_planes(own, 0), swap_planes(own, 1))
    return planes + tuple(swap_rows(p, 0) for p in planes) + (edge_own, edge_even, edge_odd)


def by_rows(values):
    return values[:, 0].transpose(1, 0, 2)


def forward_weights(weight):
    outs, taps, ins = weight.shape
    return weight.reshape(outs, 3, 3, 3, ins).transpose(3, 0, 2, 1, 4).reshape(3 * outs, 9 * ins)


def backward_weights(weight):
    outs, taps, ins = weight.shape
    turned = jnp.flip(weight.reshape(outs, 3, 3, 3, ins), axis=(1, 2, 3))
    return turned.transpose(3, 4, 2, 1, 0).reshape(3 * ins, 9 * outs)


def reduced(where, send, keep, tap_of, factor, shape):
    taps, half, width = keep.shape
    parts = lax.axis_size("cin")
    arrived = swap_rows(send, 0)
    quarter = half // 2
    send, keep = call(
        add_kernel,
        "add_halves",
        [SMEM, VMEM, VMEM],
        [struct((taps, quarter, width), BF16), struct((taps, quarter, width), F32)],
        (where, keep, arrived),
    )
    count = lax.axis_size("cout")
    arrived = lax.ppermute(send, "cout", [(i, i ^ 2) for i in range(count)])
    lanes = 128
    tiles = -(-len(tap_of) // parts)
    piece = (tiles, quarter, lanes)
    *sends, keep = call(
        pack_kernel,
        "pack_parts",
        [SMEM, VMEM, VMEM],
        [struct(piece, BF16)] * (parts - 1) + [struct(piece, F32)],
        (where, keep, arrived),
        [pltpu.VMEM((parts, *piece), F32)],
    )
    arrived = [
        lax.ppermute(value, "cin", [(i, i ^ (k + 1)) for i in range(parts)])
        for k, value in enumerate(sends)
    ]
    return call(
        functools.partial(finish_kernel, tap_of, factor),
        "finish_sum",
        [VMEM] * parts,
        [struct(shape, F32)],
        (keep, *arrived),
    )[0]


def scattered(grads, factor):
    part = lax.psum_scatter(grads, "cin", scatter_dimension=2, tiled=True)
    return lax.psum_scatter(part, "cout", scatter_dimension=0, tiled=True) * factor


def body(volume, first_filter, second_filter, cotangent):
    chans, planes, rows, width = volume.shape
    outs, taps, ins = second_filter.shape
    assert planes == 1 and outs == chans == ins
    plane_count = lax.axis_size("cin")
    row_count = lax.axis_size("cout")
    factor = 1.0 / math.sqrt(plane_count * planes * row_count * rows * width)
    plane_at = lax.axis_index("cin")
    row_at = lax.axis_index("cout")
    where = jnp.stack([plane_at % 2, row_at % 2, row_at // 2, plane_at]).astype(jnp.int32)
    pairwise = plane_count == 4 and row_count == 4
    flops = 2 * 27 * chans * chans * rows * width

    own = by_rows(volume)
    grad_own = by_rows(cotangent)
    edge_at = where[1] * (rows - 1)
    edges = jnp.stack(
        [
            lax.dynamic_index_in_dim(own, edge_at, 0, False),
            lax.dynamic_index_in_dim(grad_own, edge_at, 0, False),
        ]
    )
    edge_own = swap_rows(edges, 1)
    edge_even = swap_corner(edges, 0)
    edge_odd = swap_corner(edges, 1)
    slabs = slabs_of(own, edge_own[0], edge_even[0], edge_odd[0])
    grad_slabs = slabs_of(grad_own, edge_own[1], edge_even[1], edge_odd[1])

    field_shape = struct((rows + 2, 3, chans, width), BF16)
    slab_shape = struct((rows, chans, width), BF16)
    sems = pltpu.SemaphoreType.DMA((9,))
    field, hidden, slope, edge = call(
        first_kernel,
        "first_conv",
        [SMEM] + [ANY] * 9 + [VMEM],
        [field_shape, slab_shape, struct((rows, chans, width), F32), struct((chans, width), BF16)],
        (where, *slabs, forward_weights(first_filter)),
        [sems],
        flops,
    )

    def partials(shape):
        if not pairwise:
            return [struct(shape, F32)]
        half = (shape[0], shape[1] // 2, shape[2])
        return [struct(half, BF16), struct(half, F32)]

    second_total = (9, outs, 3 * ins)
    grad_field, *second_part = call(
        second_grad_kernel,
        "second_filter_grad",
        [SMEM] + [ANY] * 9 + [VMEM],
        [field_shape] + partials(second_total),
        (where, *grad_slabs, hidden),
        [pltpu.VMEM(second_total, F32), sems],
        flops,
    )
    first_total = (3, outs, 9 * ins)
    first_part = call(
        first_grad_kernel,
        "first_filter_grad",
        [SMEM] + [VMEM] * 4,
        partials(first_total),
        (where, backward_weights(second_filter), grad_field, slope, field),
        [pltpu.VMEM(first_total, F32)],
        2 * flops,
    )
    hidden_slabs = slabs_of(
        hidden, swap_rows(edge, 1), swap_corner(edge, 0), swap_corner(edge, 1)
    )
    (second_out,) = call(
        second_kernel,
        "second_conv",
        [SMEM] + [ANY] * 9 + [VMEM],
        [slab_shape],
        (where, *hidden_slabs, forward_weights(second_filter)),
        [pltpu.VMEM(field_shape.shape, BF16), sems],
        flops,
    )
    second_out = second_out.transpose(1, 0, 2)[:, None]

    shape = (outs // row_count, taps, ins // plane_count)
    if pairwise:
        second_taps = [26 - (a * 9 + b * 3 + e) for b in range(3) for a in range(3) for e in range(3)]
        first_taps = [a * 9 + b * 3 + e for e in range(3) for b in range(3) for a in range(3)]
        second_sum = reduced(where, *second_part, second_taps, factor, shape)
        first_sum = reduced(where, *first_part, first_taps, factor, shape)
    else:
        second_grads = second_part[0].reshape(3, 3, outs, 3, ins).transpose(2, 1, 0, 3, 4)
        second_grads = jnp.flip(second_grads, axis=(1, 2, 3)).reshape(outs, taps, ins)
        first_grads = first_part[0].reshape(3, outs, 3, 3, ins).transpose(1, 3, 2, 0, 4)
        first_grads = first_grads.reshape(outs, taps, ins)
        second_sum = scattered(second_grads, factor)
        first_sum = scattered(first_grads, factor)
    return (second_out, first_sum, second_sum)


def solution(mesh):
    return jax.shard_map(
        body,
        mesh=mesh,
        in_specs=(
            P(None, ("grp", "cin"), "cout", None),
            P(),
            P(),
            P(None, ("grp", "cin"), "cout", None),
        ),
        out_specs=(
            P(None, ("grp", "cin"), "cout", None),
            P("cout", "grp", "cin"),
            P("cout", "grp", "cin"),
        ),
        check_vma=False,
    )
```

```python
import functools
import math

import jax
import jax.numpy as jnp
from jax import lax
from jax.experimental import pallas as pl
from jax.experimental.pallas import tpu as pltpu
from jax.sharding import PartitionSpec as P

VMEM = pl.BlockSpec(memory_space=pltpu.VMEM)
SMEM = pl.BlockSpec(memory_space=pltpu.SMEM)
F32 = jnp.float32
BF16 = jnp.bfloat16
LIMIT = 14 * 1024 * 1024


def links(count, odd):
    pairs = []
    for i in range(odd, count - 1, 2):
        pairs += [(i, i + 1), (i + 1, i)]
    return pairs


def swap_planes(values, odd):
    return lax.ppermute(values, "cin", links(lax.axis_size("cin"), odd))


def swap_rows(values, odd):
    return lax.ppermute(values, "cout", links(lax.axis_size("cout"), odd))


def swap_corner(values, odd):
    count = lax.axis_size("cout")
    pairs = [
        (a * count + c, b * count + d)
        for a, b in links(lax.axis_size("cin"), odd)
        for c, d in links(count, 1)
    ]
    return lax.ppermute(values, ("cin", "cout"), pairs)


def shift_up(values):
    lane = lax.broadcasted_iota(jnp.int32, values.shape, 1)
    return jnp.where(lane == 0, 0.0, pltpu.roll(values, 1, 1))


def shift_down(values):
    width = values.shape[1]
    lane = lax.broadcasted_iota(jnp.int32, values.shape, 1)
    return jnp.where(lane == width - 1, 0.0, pltpu.roll(values, width - 1, 1))


def spread(values):
    wide = values.astype(F32)
    return jnp.concatenate(
        [shift_down(wide).astype(BF16), values, shift_up(wide).astype(BF16)], axis=0
    )


def combine(products):
    chans = products.shape[0] // 3
    return (
        products[chans : 2 * chans]
        + shift_up(products[:chans])
        + shift_down(products[2 * chans :])
    )


def planes_of(where):
    return (1, 2 * (1 - where[0]), 2 * where[0])


def fill(where, slabs, edges, field):
    rows = slabs[0].shape[0]
    row = where[1]
    for k, plane in enumerate(planes_of(where)):
        for r in range(rows):
            field[1 + r, plane] = slabs[k][r]
        field[(1 - row) * (rows + 1), plane] = slabs[3 + k][row * (rows - 1)]
        field[row * (rows + 1), plane] = edges[k][...]


def halves(where, quarter):
    mine = where[1]
    return [pl.ds(pl.multiple_of(2 * h * quarter + mine * quarter, quarter), quarter) for h in range(2)]


def fill_pair(where, slabs, edges, pair_edges, field, split):
    rows = slabs[0].shape[0]
    row = where[1]

    def put(at, plane, value):
        if not split:
            field[at, plane] = value[...]
            return
        quarter = field.shape[2] // 2
        for h, part in enumerate(halves(where, quarter)):
            field[at, plane, h * quarter : (h + 1) * quarter] = value[part]

    for k, plane in enumerate(planes_of(where)):
        for r in range(rows):
            put(1 + row * rows + r, plane, slabs[k].at[r])
            put(1 + (1 - row) * rows + r, plane, slabs[3 + k].at[r])
        put(row * (2 * rows + 1), plane, edges[k])
        put((1 - row) * (2 * rows + 1), plane, pair_edges[k])


def window(field, row):
    block = field[row : row + 3]
    return block.reshape(-1, block.shape[-1])


def conv_rows(weights, field, row):
    return combine(jnp.dot(weights[...], window(field, row), preferred_element_type=F32))


def prepare_kernel(values, out):
    out[...] = jnp.transpose(values[:, 0], (1, 0, 2))


def prepare_pair_kernel(where, values, other, out, edges):
    out[...] = jnp.transpose(values[:, 0], (1, 0, 2))
    at = where[1] * (out.shape[0] - 1)
    edges[0] = other[at]
    edges[1] = out[at]


def edge_kernel(where, *refs):
    out = refs[-1]
    for k, slab in enumerate(refs[:-1]):
        out[k] = slab[where[1] * (slab.shape[0] - 1)]


def weights_kernel(first, second, first_out, second_out, back_out):
    chans = first.shape[1]
    for b in range(3):
        for a in range(3):
            for e in range(3):
                tap = a * 9 + b * 3 + e
                at = (
                    slice(e * chans, (e + 1) * chans),
                    slice((b * 3 + a) * chans, (b * 3 + a + 1) * chans),
                )
                first_out[at] = first[tap]
                second_out[at] = second[tap]
                back_out[at] = second[26 - tap].T


def first_kernel(where, *refs):
    slabs = refs[:6]
    edges = [ref.at[0] for ref in refs[6:9]]
    weights, hidden, slope, field = refs[9:]
    fill(where, slabs, edges, field)
    for row in range(hidden.shape[0]):
        value = conv_rows(weights, field, row)
        gate = 1.0 / (1.0 + jnp.exp(-value))
        hidden[row] = (value * gate).astype(BF16)
        slope[row] = gate * (1.0 + value * (1.0 - gate))


def second_kernel(where, *refs):
    slabs = refs[:6]
    packed, weights, out, field, held = refs[6:]
    fill(where, slabs, [packed.at[k] for k in range(3)], field)
    for row in range(held.shape[0]):
        held[row] = conv_rows(weights, field, row).astype(BF16)
    out[:, 0] = jnp.transpose(held[...], (1, 0, 2))


def grad_kernel(where, *refs):
    slabs = refs[:6]
    edges = [ref.at[1] for ref in refs[6:9]]
    weights, slope, keep, *rest = refs[9:]
    *send, field, whole = rest
    fill(where, slabs, edges, field)
    for row in range(slope.shape[0]):
        grad = (conv_rows(weights, field, row) * slope[row]).astype(BF16)
        if not send:
            keep[row] = grad
        else:
            whole[...] = grad
            quarter = keep.shape[1] // 2
            for h in range(2):
                at = pl.ds(h * quarter, quarter)
                mine = pl.ds(pl.multiple_of((2 * h + where[1]) * quarter, quarter), quarter)
                theirs = pl.ds(pl.multiple_of((2 * h + 1 - where[1]) * quarter, quarter), quarter)
                keep[row, at] = whole[mine]
                send[0][row, at] = whole[theirs]


def pair_off(where, total, send, keep):
    width = send.shape[1]
    mine = pl.multiple_of(where[2] * width, width)
    theirs = pl.multiple_of((1 - where[2]) * width, width)
    send[...] = total[:, pl.ds(theirs, width)].astype(BF16)
    keep[...] = total[:, pl.ds(mine, width)]


def ordered(where, own, pair, both):
    rows = own.shape[0]
    for r in range(rows):
        both[where[1] * rows + r] = own[r]
        both[(1 - where[1]) * rows + r] = pair[r]


def second_grad_kernel(where, *refs):
    slabs = refs[:6]
    edges = [ref.at[1] for ref in refs[6:9]]
    pair_edges = [ref.at[1] for ref in refs[9:12]]
    hidden, pair_hidden, send, keep, field, both, total = refs[12:]
    fill_pair(where, slabs, edges, pair_edges, field, True)
    ordered(where, hidden, pair_hidden, both)
    for row in range(both.shape[0]):
        part = lax.dot_general(
            window(field, row),
            spread(both[row]),
            (((1,), (1,)), ((), ())),
            preferred_element_type=F32,
        ).reshape(total.shape)
        total[...] = part if row == 0 else total[...] + part
    pair_off(where, total, send, keep)


def first_grad_kernel(where, *refs):
    slabs = refs[:6]
    edges = [ref.at[0] for ref in refs[6:9]]
    pair_edges = [ref.at[0] for ref in refs[9:12]]
    grad, pair_grad, send, keep, field, both, total = refs[12:]
    fill_pair(where, slabs, edges, pair_edges, field, False)
    ordered(where, grad, pair_grad, both)
    for row in range(both.shape[0]):
        part = lax.dot_general(
            spread(both[row]),
            window(field, row),
            (((1,), (1,)), ((), ())),
            preferred_element_type=F32,
        ).reshape(total.shape)
        total[...] = part if row == 0 else total[...] + part
    pair_off(where, total, send, keep)


def second_total_kernel(where, *refs):
    slabs = refs[:6]
    edges = [ref.at[1] for ref in refs[6:9]]
    hidden, total, field = refs[9:]
    fill(where, slabs, edges, field)
    for row in range(hidden.shape[0]):
        part = lax.dot_general(
            window(field, row),
            spread(hidden[row]),
            (((1,), (1,)), ((), ())),
            preferred_element_type=F32,
        ).reshape(total.shape)
        total[...] = part if row == 0 else total[...] + part


def first_total_kernel(where, *refs):
    slabs = refs[:6]
    edges = [ref.at[0] for ref in refs[6:9]]
    grad, total, field = refs[9:]
    fill(where, slabs, edges, field)
    for row in range(grad.shape[0]):
        part = lax.dot_general(
            spread(grad[row]),
            window(field, row),
            (((1,), (1,)), ((), ())),
            preferred_element_type=F32,
        ).reshape(total.shape)
        total[...] = part if row == 0 else total[...] + part


def pack_kernel(where, held, arrived, *refs):
    sends = refs[:-2]
    keep, packed = refs[-2:]
    parts, tiles, outs, lanes = packed.shape
    group = lanes // parts
    per = held.shape[2] // lanes
    sums = {}
    for n in range(held.shape[0] * per):
        at = (n // per, slice(None), slice(n % per * lanes, (n % per + 1) * lanes))
        sums[n] = held[at] + arrived[at].astype(F32)
    lane = lax.broadcasted_iota(jnp.int32, (outs, lanes), 1) // group
    for tile in range(tiles):
        for part in range(parts):
            value = jnp.zeros((outs, lanes), F32)
            for place in range(parts):
                n = tile * parts + place
                if n in sums:
                    turned = sums[n]
                    if place != part:
                        turned = pltpu.roll(turned, (place - part) % parts * group, 1)
                    value = jnp.where(lane == place, turned, value)
            packed[part, tile] = value
    mine = where[3]
    keep[...] = packed[mine]
    for k, send in enumerate(sends):
        send[...] = packed[mine ^ (k + 1)].astype(BF16)


def finish_kernel(tap_of, factor, held, *refs):
    out = refs[-1]
    tiles, outs, lanes = held.shape
    group = out.shape[2]
    places = lanes // group
    for tile in range(tiles):
        total = held[tile]
        for arrived in refs[:-1]:
            total = total + arrived[tile].astype(F32)
        total = total * factor
        for place in range(places):
            n = tile * places + place
            if n < len(tap_of):
                out[tap_of[n]] = total[:, place * group : (place + 1) * group]


def struct(shape, dtype):
    return jax.ShapeDtypeStruct(shape, dtype)


def call(kernel, name, out_shapes, args, scratch=(), flops=0, scalars=True):
    moved = sum(math.prod(a.shape) * a.dtype.itemsize for a in (*args, *out_shapes))
    return pl.pallas_call(
        kernel,
        name=name,
        in_specs=[SMEM] * scalars + [VMEM] * (len(args) - scalars),
        out_specs=[VMEM] * len(out_shapes),
        out_shape=out_shapes,
        scratch_shapes=[pltpu.VMEM(s.shape, s.dtype) for s in scratch],
        cost_estimate=pl.CostEstimate(flops=flops, bytes_accessed=moved, transcendentals=0),
        compiler_params=pltpu.CompilerParams(vmem_limit_bytes=LIMIT),
    )(*args)


def slabs_of(own):
    planes = (own, swap_planes(own, 0), swap_planes(own, 1))
    return planes + tuple(swap_rows(p, 0) for p in planes)


def reduced(where, send, keep, tap_of, factor, shape):
    taps, outs, width = keep.shape
    parts = lax.axis_size("cin")
    count = lax.axis_size("cout")
    arrived = lax.ppermute(send, "cout", [(i, i ^ 2) for i in range(count)])
    lanes = 128
    tiles = -(-len(tap_of) // parts)
    piece = (tiles, outs, lanes)
    *sends, keep = call(
        pack_kernel,
        "pack_parts",
        [struct(piece, BF16)] * (parts - 1) + [struct(piece, F32)],
        (where, keep, arrived),
        [struct((parts, *piece), F32)],
    )
    arrived = [
        lax.ppermute(value, "cin", [(i, i ^ (k + 1)) for i in range(parts)])
        for k, value in enumerate(sends)
    ]
    (total,) = call(
        functools.partial(finish_kernel, tap_of, factor),
        "finish_sum",
        [struct((shape[1], shape[0], shape[2]), F32)],
        (keep, *arrived),
        scalars=False,
    )
    return total.transpose(1, 0, 2)


def scattered(grads, factor):
    part = lax.psum_scatter(grads, "cin", scatter_dimension=2, tiled=True)
    return lax.psum_scatter(part, "cout", scatter_dimension=0, tiled=True) * factor


def body(volume, first_filter, second_filter, cotangent):
    chans, planes, rows, width = volume.shape
    outs, taps, ins = second_filter.shape
    assert planes == 1 and outs == chans == ins
    plane_count = lax.axis_size("cin")
    row_count = lax.axis_size("cout")
    factor = 1.0 / math.sqrt(plane_count * planes * row_count * rows * width)
    plane_at = lax.axis_index("cin")
    row_at = lax.axis_index("cout")
    where = jnp.stack([plane_at % 2, row_at % 2, row_at // 2, plane_at]).astype(jnp.int32)
    pairwise = plane_count == 4 and row_count == 4
    flops = 2 * 27 * chans * chans * rows * width
    slab = struct((rows, chans, width), BF16)
    field = struct((rows + 2, 3, chans, width), BF16)
    matrix = struct((3 * chans, 9 * chans), BF16)

    (own,) = call(prepare_kernel, "prepare_volume", [slab], (volume,), scalars=False)
    grad_own, edge = call(
        prepare_pair_kernel,
        "prepare_cotangent",
        [slab, struct((2, chans, width), BF16)],
        (where, cotangent, own),
    )
    slabs = slabs_of(own)
    edges = (swap_rows(edge, 1), swap_corner(edge, 0), swap_corner(edge, 1))
    grad_slabs = slabs_of(grad_own)
    first_weights, second_weights, back_weights = call(
        weights_kernel,
        "weights",
        [matrix] * 3,
        (first_filter.transpose(1, 0, 2), second_filter.transpose(1, 0, 2)),
        scalars=False,
    )
    hidden, slope = call(
        first_kernel,
        "first_conv",
        [slab, struct(slab.shape, F32)],
        (where, *slabs, *edges, first_weights),
        [field],
        flops,
    )
    half = struct((rows, chans // 2, width), BF16)
    grads = call(
        grad_kernel,
        "hidden_grad",
        [half, half] if pairwise else [slab],
        (where, *grad_slabs, *edges, back_weights, slope),
        [field, struct((chans, width), BF16)],
        flops,
    )
    shape = (outs // row_count, taps, ins // plane_count)
    hidden_slabs = slabs_of(hidden)
    if pairwise:
        pair_edges = tuple(swap_rows(e, 0) for e in edges)
        wide = 2 * rows + 2
        block = shape[0]
        second_part = call(
            second_grad_kernel,
            "second_filter_grad",
            [struct((9, block, 3 * ins), BF16), struct((9, block, 3 * ins), F32)],
            (where, *grad_slabs, *edges, *pair_edges, hidden, hidden_slabs[3]),
            [
                struct((wide, 3, 2 * block, width), BF16),
                struct((2 * rows, chans, width), BF16),
                struct((9, 2 * block, 3 * ins), F32),
            ],
            flops,
        )
        first_part = call(
            first_grad_kernel,
            "first_filter_grad",
            [struct((3, block, 9 * ins), BF16), struct((3, block, 9 * ins), F32)],
            (where, *slabs, *edges, *pair_edges, grads[0], swap_rows(grads[1], 0)),
            [
                struct((wide, 3, chans, width), BF16),
                struct((2 * rows, 2 * block, width), BF16),
                struct((3, 2 * block, 9 * ins), F32),
            ],
            flops,
        )
        steps = range(3)
        second_taps = [26 - (a * 9 + b * 3 + e) for b in steps for a in steps for e in steps]
        first_taps = [a * 9 + b * 3 + e for e in steps for b in steps for a in steps]
        second_sum = reduced(where, *second_part, second_taps, factor, shape)
        first_sum = reduced(where, *first_part, first_taps, factor, shape)
    else:
        (second_total,) = call(
            second_total_kernel,
            "second_filter_grad",
            [struct((9, outs, 3 * ins), F32)],
            (where, *grad_slabs, *edges, hidden),
            [field],
            flops,
        )
        (first_total,) = call(
            first_total_kernel,
            "first_filter_grad",
            [struct((3, outs, 9 * ins), F32)],
            (where, *slabs, *edges, *grads),
            [field],
            flops,
        )
        second_total = second_total.reshape(3, 3, outs, 3, ins).transpose(2, 1, 0, 3, 4)
        second_total = jnp.flip(second_total, axis=(1, 2, 3)).reshape(outs, taps, ins)
        first_total = first_total.reshape(3, outs, 3, 3, ins).transpose(1, 3, 2, 0, 4)
        second_sum = scattered(second_total, factor)
        first_sum = scattered(first_total.reshape(outs, taps, ins), factor)

    (packed,) = call(
        edge_kernel, "hidden_edges", [struct((3, chans, width), BF16)], (where, *hidden_slabs[:3])
    )
    (second_out,) = call(
        second_kernel,
        "second_conv",
        [struct(volume.shape, BF16)],
        (where, *hidden_slabs, swap_rows(packed, 1), second_weights),
        [field, slab],
        flops,
    )
    return (second_out, first_sum, second_sum)


def solution(mesh):
    return jax.shard_map(
        body,
        mesh=mesh,
        in_specs=(
            P(None, ("grp", "cin"), "cout", None),
            P(),
            P(),
            P(None, ("grp", "cin"), "cout", None),
        ),
        out_specs=(
            P(None, ("grp", "cin"), "cout", None),
            P("cout", "grp", "cin"),
            P("cout", "grp", "cin"),
        ),
        check_vma=False,
    )
```

```python
import functools
import math

import jax
import jax.numpy as jnp
from jax import lax
from jax.experimental import pallas as pl
from jax.experimental.pallas import tpu as pltpu
from jax.sharding import PartitionSpec as P

VMEM = pl.BlockSpec(memory_space=pltpu.VMEM)
SMEM = pl.BlockSpec(memory_space=pltpu.SMEM)
F32 = jnp.float32
BF16 = jnp.bfloat16
LIMIT = 14 * 1024 * 1024


def links(count, odd):
    pairs = []
    for i in range(odd, count - 1, 2):
        pairs += [(i, i + 1), (i + 1, i)]
    return pairs


def swap_planes(values, odd):
    return lax.ppermute(values, "cin", links(lax.axis_size("cin"), odd))


def swap_rows(values, odd):
    return lax.ppermute(values, "cout", links(lax.axis_size("cout"), odd))


def shift_up(values):
    lane = lax.broadcasted_iota(jnp.int32, values.shape, 1)
    return jnp.where(lane == 0, 0.0, pltpu.roll(values, 1, 1))


def shift_down(values):
    width = values.shape[1]
    lane = lax.broadcasted_iota(jnp.int32, values.shape, 1)
    return jnp.where(lane == width - 1, 0.0, pltpu.roll(values, width - 1, 1))


def spread(values):
    wide = values.astype(F32)
    return jnp.concatenate(
        [shift_down(wide).astype(BF16), values, shift_up(wide).astype(BF16)], axis=0
    )


def combine(products):
    chans = products.shape[0] // 3
    return (
        products[chans : 2 * chans]
        + shift_up(products[:chans])
        + shift_down(products[2 * chans :])
    )


def planes_of(where):
    return (1, 2 * (1 - where[0]), 2 * where[0])


def fill(where, slabs, edges, field):
    rows = slabs[0].shape[0]
    row = where[1]
    for k, plane in enumerate(planes_of(where)):
        for r in range(rows):
            field[1 + r, plane] = slabs[k][r]
        inside = slabs[3 + k][row * (rows - 1)] if len(slabs) == 6 else slabs[3][k]
        field[(1 - row) * (rows + 1), plane] = inside
        field[row * (rows + 1), plane] = edges[k]


def halves(where, quarter):
    mine = where[1]
    return [pl.ds(pl.multiple_of(2 * h * quarter + mine * quarter, quarter), quarter) for h in range(2)]


def fill_pair(where, slabs, edges, pair_edges, field, split):
    rows = slabs[0].shape[0]
    row = where[1]

    def put(at, plane, value):
        if not split:
            field[at, plane] = value[...]
            return
        quarter = field.shape[2] // 2
        for h, part in enumerate(halves(where, quarter)):
            field[at, plane, h * quarter : (h + 1) * quarter] = value[part]

    for k, plane in enumerate(planes_of(where)):
        for r in range(rows):
            put(1 + row * rows + r, plane, slabs[k].at[r])
            put(1 + (1 - row) * rows + r, plane, slabs[3 + k].at[r])
        put(row * (2 * rows + 1), plane, edges.at[k])
        put((1 - row) * (2 * rows + 1), plane, pair_edges.at[k])


def window(field, row):
    block = field[row : row + 3]
    return block.reshape(-1, block.shape[-1])


def conv_rows(weights, field, row):
    return combine(jnp.dot(weights[...], window(field, row), preferred_element_type=F32))


def prepare_kernel(values, out):
    out[...] = jnp.transpose(values[:, 0], (1, 0, 2))


def edge_kernel(where, own, even, odd, across, *inside):
    last = own.shape[0] - 1
    for k, slab in enumerate((own, even, odd)):
        across[k] = slab[where[1] * last]
        for out in inside:
            out[k] = slab[(1 - where[1]) * last]


def weights_kernel(first, second, first_out, second_out, back_out):
    chans = first.shape[1]
    for b in range(3):
        for a in range(3):
            for e in range(3):
                tap = a * 9 + b * 3 + e
                at = (
                    slice(e * chans, (e + 1) * chans),
                    slice((b * 3 + a) * chans, (b * 3 + a + 1) * chans),
                )
                first_out[at] = first[tap]
                second_out[at] = second[tap]
                back_out[at] = second[26 - tap].T


def first_kernel(where, *refs):
    slabs = refs[:6]
    edges, weights, hidden, slope, field = refs[6:]
    fill(where, slabs, edges, field)
    for row in range(hidden.shape[0]):
        value = conv_rows(weights, field, row)
        gate = 1.0 / (1.0 + jnp.exp(-value))
        hidden[row] = (value * gate).astype(BF16)
        slope[row] = gate * (1.0 + value * (1.0 - gate))


def second_kernel(where, *refs):
    slabs = refs[:4]
    packed, weights, out, field, held = refs[4:]
    fill(where, slabs, packed, field)
    for row in range(held.shape[0]):
        held[row] = conv_rows(weights, field, row).astype(BF16)
    out[:, 0] = jnp.transpose(held[...], (1, 0, 2))


def grad_kernel(where, *refs):
    slabs = refs[:6]
    edges, weights, slope, keep, *rest = refs[6:]
    *send, field, whole = rest
    fill(where, slabs, edges, field)
    for row in range(slope.shape[0]):
        grad = (conv_rows(weights, field, row) * slope[row]).astype(BF16)
        if not send:
            keep[row] = grad
        else:
            whole[...] = grad
            quarter = keep.shape[1] // 2
            for h in range(2):
                at = pl.ds(h * quarter, quarter)
                mine = pl.ds(pl.multiple_of((2 * h + where[1]) * quarter, quarter), quarter)
                theirs = pl.ds(pl.multiple_of((2 * h + 1 - where[1]) * quarter, quarter), quarter)
                keep[row, at] = whole[mine]
                send[0][row, at] = whole[theirs]


def pair_off(where, total, send, keep):
    width = send.shape[1]
    mine = pl.multiple_of(where[2] * width, width)
    theirs = pl.multiple_of((1 - where[2]) * width, width)
    send[...] = total[:, pl.ds(theirs, width)].astype(BF16)
    keep[...] = total[:, pl.ds(mine, width)]


def ordered(where, own, pair, both):
    rows = own.shape[0]
    for r in range(rows):
        both[where[1] * rows + r] = own[r]
        both[(1 - where[1]) * rows + r] = pair[r]


def second_grad_kernel(where, *refs):
    slabs = refs[:6]
    edges, pair_edges, hidden, pair_hidden, send, keep, field, both, total = refs[6:]
    fill_pair(where, slabs, edges, pair_edges, field, True)
    ordered(where, hidden, pair_hidden, both)
    for row in range(both.shape[0]):
        part = lax.dot_general(
            window(field, row),
            spread(both[row]),
            (((1,), (1,)), ((), ())),
            preferred_element_type=F32,
        ).reshape(total.shape)
        total[...] = part if row == 0 else total[...] + part
    pair_off(where, total, send, keep)


def first_grad_kernel(where, *refs):
    slabs = refs[:6]
    edges, pair_edges, grad, pair_grad, send, keep, field, both, total = refs[6:]
    fill_pair(where, slabs, edges, pair_edges, field, False)
    ordered(where, grad, pair_grad, both)
    for row in range(both.shape[0]):
        part = lax.dot_general(
            spread(both[row]),
            window(field, row),
            (((1,), (1,)), ((), ())),
            preferred_element_type=F32,
        ).reshape(total.shape)
        total[...] = part if row == 0 else total[...] + part
    pair_off(where, total, send, keep)


def second_total_kernel(where, *refs):
    slabs = refs[:6]
    edges, hidden, total, field = refs[6:]
    fill(where, slabs, edges, field)
    for row in range(hidden.shape[0]):
        part = lax.dot_general(
            window(field, row),
            spread(hidden[row]),
            (((1,), (1,)), ((), ())),
            preferred_element_type=F32,
        ).reshape(total.shape)
        total[...] = part if row == 0 else total[...] + part


def first_total_kernel(where, *refs):
    slabs = refs[:6]
    edges, grad, total, field = refs[6:]
    fill(where, slabs, edges, field)
    for row in range(grad.shape[0]):
        part = lax.dot_general(
            spread(grad[row]),
            window(field, row),
            (((1,), (1,)), ((), ())),
            preferred_element_type=F32,
        ).reshape(total.shape)
        total[...] = part if row == 0 else total[...] + part


def pack_kernel(where, held, arrived, *refs):
    sends = refs[:-2]
    keep, packed = refs[-2:]
    parts, tiles, outs, lanes = packed.shape
    group = lanes // parts
    per = held.shape[2] // lanes
    sums = {}
    for n in range(held.shape[0] * per):
        at = (n // per, slice(None), slice(n % per * lanes, (n % per + 1) * lanes))
        sums[n] = held[at] + arrived[at].astype(F32)
    lane = lax.broadcasted_iota(jnp.int32, (outs, lanes), 1) // group
    for tile in range(tiles):
        for part in range(parts):
            value = jnp.zeros((outs, lanes), F32)
            for place in range(parts):
                n = tile * parts + place
                if n in sums:
                    turned = sums[n]
                    if place != part:
                        turned = pltpu.roll(turned, (place - part) % parts * group, 1)
                    value = jnp.where(lane == place, turned, value)
            packed[part, tile] = value
    mine = where[3]
    keep[...] = packed[mine]
    for k, send in enumerate(sends):
        send[...] = packed[mine ^ (k + 1)].astype(BF16)


def finish_kernel(tap_of, factor, held, *refs):
    out = refs[-1]
    tiles, outs, lanes = held.shape
    group = out.shape[2]
    places = lanes // group
    for tile in range(tiles):
        total = held[tile]
        for arrived in refs[:-1]:
            total = total + arrived[tile].astype(F32)
        total = total * factor
        for place in range(places):
            n = tile * places + place
            if n < len(tap_of):
                out[tap_of[n]] = total[:, place * group : (place + 1) * group]


def struct(shape, dtype):
    return jax.ShapeDtypeStruct(shape, dtype)


def call(kernel, name, out_shapes, args, scratch=(), flops=0, scalars=True):
    moved = sum(math.prod(a.shape) * a.dtype.itemsize for a in (*args, *out_shapes))
    return pl.pallas_call(
        kernel,
        name=name,
        in_specs=[SMEM] * scalars + [VMEM] * (len(args) - scalars),
        out_specs=[VMEM] * len(out_shapes),
        out_shape=out_shapes,
        scratch_shapes=[pltpu.VMEM(s.shape, s.dtype) for s in scratch],
        cost_estimate=pl.CostEstimate(flops=flops, bytes_accessed=moved, transcendentals=0),
        compiler_params=pltpu.CompilerParams(vmem_limit_bytes=LIMIT),
    )(*args)


def after(value, *others):
    return lax.optimization_barrier((value, *others))[0]


def packed_parts(where, keep, arrived):
    taps, outs, width = keep.shape
    parts = lax.axis_size("cin")
    lanes = 128
    tiles = -(-taps * width // (lanes * parts))
    piece = (tiles, outs, lanes)
    return call(
        pack_kernel,
        "pack_parts",
        [struct(piece, BF16)] * (parts - 1) + [struct(piece, F32)],
        (where, keep, arrived),
        [struct((parts, *piece), F32)],
    )


def exchanged(sends):
    parts = lax.axis_size("cin")
    return [
        lax.ppermute(value, "cin", [(i, i ^ (k + 1)) for i in range(parts)])
        for k, value in enumerate(sends)
    ]


def finished(keep, arrived, tap_of, factor, shape):
    (total,) = call(
        functools.partial(finish_kernel, tap_of, factor),
        "finish_sum",
        [struct((shape[1], shape[0], shape[2]), F32)],
        (keep, *arrived),
        scalars=False,
    )
    return total.transpose(1, 0, 2)


def cross(values):
    return lax.ppermute(values, "cout", [(i, i ^ 2) for i in range(lax.axis_size("cout"))])


def scattered(grads, factor):
    part = lax.psum_scatter(grads, "cin", scatter_dimension=2, tiled=True)
    return lax.psum_scatter(part, "cout", scatter_dimension=0, tiled=True) * factor


def body(volume, first_filter, second_filter, cotangent):
    chans, planes, rows, width = volume.shape
    outs, taps, ins = second_filter.shape
    assert planes == 1 and outs == chans == ins
    plane_count = lax.axis_size("cin")
    row_count = lax.axis_size("cout")
    factor = 1.0 / math.sqrt(plane_count * planes * row_count * rows * width)
    plane_at = lax.axis_index("cin")
    row_at = lax.axis_index("cout")
    where = jnp.stack([plane_at % 2, row_at % 2, row_at // 2, plane_at]).astype(jnp.int32)
    pairwise = plane_count == 4 and row_count == 4
    flops = 2 * 27 * chans * chans * rows * width
    slab = struct((rows, chans, width), BF16)
    field = struct((rows + 2, 3, chans, width), BF16)
    matrix = struct((3 * chans, 9 * chans), BF16)

    (own,) = call(prepare_kernel, "prepare_volume", [slab], (volume,), scalars=False)
    own_even, own_odd, own_pair = swap_planes(own, 0), swap_planes(own, 1), swap_rows(own, 0)
    (grad_own,) = call(
        prepare_kernel, "prepare_cotangent", [slab], (cotangent,), scalars=False
    )
    grad_even, grad_odd = swap_planes(grad_own, 0), swap_planes(grad_own, 1)
    first_weights, second_weights, back_weights = call(
        weights_kernel,
        "weights",
        [matrix] * 3,
        (first_filter.transpose(1, 0, 2), second_filter.transpose(1, 0, 2)),
        scalars=False,
    )

    def across(own, even, odd):
        (out,) = call(
            edge_kernel,
            "edges",
            [struct((3, chans, width), BF16)],
            (where, own, even, odd),
        )
        return swap_rows(out, 1)

    edges = across(own, after(own_even, first_weights), own_odd)
    slabs = (own, own_even, own_odd, own_pair, swap_rows(own_even, 0), swap_rows(own_odd, 0))
    hidden, slope = call(
        first_kernel,
        "first_conv",
        [slab, struct(slab.shape, F32)],
        (where, *slabs, edges, first_weights),
        [field],
        flops,
    )
    hidden_pair = swap_rows(hidden, 0)
    hidden_even, hidden_odd = swap_planes(hidden, 0), swap_planes(hidden, 1)
    grad_edges = across(grad_own, grad_even, grad_odd)
    grad_slabs = (
        grad_own,
        grad_even,
        grad_odd,
        swap_rows(grad_own, 0),
        swap_rows(grad_even, 0),
        swap_rows(grad_odd, 0),
    )
    half = struct((rows, chans // 2, width), BF16)
    grads = call(
        grad_kernel,
        "hidden_grad",
        [half, half] if pairwise else [slab],
        (where, *grad_slabs, grad_edges, back_weights, slope),
        [field, struct((chans, width), BF16)],
        flops,
    )
    shape = (outs // row_count, taps, ins // plane_count)

    def hidden_rows(even, odd, *others):
        across, inside = call(
            edge_kernel,
            "hidden_edges",
            [struct((3, chans, width), BF16)] * 2,
            (where, hidden, even, odd),
        )
        across, inside, *_ = lax.optimization_barrier((across, inside, *others))
        return swap_rows(inside, 0), swap_rows(across, 1)

    def convolved(inside, across):
        (out,) = call(
            second_kernel,
            "second_conv",
            [struct(volume.shape, BF16)],
            (where, hidden, hidden_even, hidden_odd, inside, across, second_weights),
            [field, slab],
            flops,
        )
        return out

    if pairwise:
        pair_edges, pair_grad_edges = swap_rows(edges, 0), swap_rows(grad_edges, 0)
        wide = 2 * rows + 2
        block = shape[0]
        second_send, second_keep = call(
            second_grad_kernel,
            "second_filter_grad",
            [struct((9, block, 3 * ins), BF16), struct((9, block, 3 * ins), F32)],
            (where, *grad_slabs, grad_edges, pair_grad_edges, hidden, hidden_pair),
            [
                struct((wide, 3, 2 * block, width), BF16),
                struct((2 * rows, chans, width), BF16),
                struct((9, 2 * block, 3 * ins), F32),
            ],
            flops,
        )
        second_arrived = cross(second_send)
        first_send, first_keep = call(
            first_grad_kernel,
            "first_filter_grad",
            [struct((3, block, 9 * ins), BF16), struct((3, block, 9 * ins), F32)],
            (
                where,
                *slabs,
                edges,
                pair_edges,
                after(grads[0], second_send),
                swap_rows(grads[1], 0),
            ),
            [
                struct((wide, 3, chans, width), BF16),
                struct((2 * rows, 2 * block, width), BF16),
                struct((3, 2 * block, 9 * ins), F32),
            ],
            flops,
        )
        first_arrived = cross(first_send)
        inside, across = hidden_rows(after(hidden_even, first_send), hidden_odd, second_arrived)
        steps = range(3)
        second_taps = [26 - (a * 9 + b * 3 + e) for b in steps for a in steps for e in steps]
        first_taps = [a * 9 + b * 3 + e for e in steps for b in steps for a in steps]
        *second_parts, second_keep = packed_parts(
            where, after(second_keep, inside), second_arrived
        )
        second_parts = exchanged(second_parts)
        *first_parts, first_keep = packed_parts(
            where, after(first_keep, second_keep), first_arrived
        )
        first_parts = exchanged(first_parts)
        second_sum = finished(
            after(second_keep, first_keep), second_parts, second_taps, factor, shape
        )
        first_sum = finished(first_keep, first_parts, first_taps, factor, shape)
        second_out = convolved(after(inside, first_keep), across)
    else:
        second_out = convolved(*hidden_rows(hidden_even, hidden_odd))
        (second_total,) = call(
            second_total_kernel,
            "second_filter_grad",
            [struct((9, outs, 3 * ins), F32)],
            (where, *grad_slabs, grad_edges, hidden),
            [field],
            flops,
        )
        (first_total,) = call(
            first_total_kernel,
            "first_filter_grad",
            [struct((3, outs, 9 * ins), F32)],
            (where, *slabs, edges, *grads),
            [field],
            flops,
        )
        second_total = second_total.reshape(3, 3, outs, 3, ins).transpose(2, 1, 0, 3, 4)
        second_total = jnp.flip(second_total, axis=(1, 2, 3)).reshape(outs, taps, ins)
        first_total = first_total.reshape(3, outs, 3, 3, ins).transpose(1, 3, 2, 0, 4)
        second_sum = scattered(second_total, factor)
        first_sum = scattered(first_total.reshape(outs, taps, ins), factor)
    return (second_out, first_sum, second_sum)


def solution(mesh):
    return jax.shard_map(
        body,
        mesh=mesh,
        in_specs=(
            P(None, ("grp", "cin"), "cout", None),
            P(),
            P(),
            P(None, ("grp", "cin"), "cout", None),
        ),
        out_specs=(
            P(None, ("grp", "cin"), "cout", None),
            P("cout", "grp", "cin"),
            P("cout", "grp", "cin"),
        ),
        check_vma=False,
    )
```

```python
import functools
import math

import jax
import jax.numpy as jnp
from jax import lax
from jax.experimental import pallas as pl
from jax.experimental.pallas import tpu as pltpu
from jax.sharding import PartitionSpec as P

VMEM = pl.BlockSpec(memory_space=pltpu.VMEM)
SMEM = pl.BlockSpec(memory_space=pltpu.SMEM)
F32 = jnp.float32
BF16 = jnp.bfloat16
LIMIT = 14 * 1024 * 1024


def links(count, odd):
    pairs = []
    for i in range(odd, count - 1, 2):
        pairs += [(i, i + 1), (i + 1, i)]
    return pairs


def swap_planes(values, odd):
    return lax.ppermute(values, "cin", links(lax.axis_size("cin"), odd))


def swap_rows(values, odd):
    return lax.ppermute(values, "cout", links(lax.axis_size("cout"), odd))


def shift_up(values):
    lane = lax.broadcasted_iota(jnp.int32, values.shape, 1)
    return jnp.where(lane == 0, 0.0, pltpu.roll(values, 1, 1))


def shift_down(values):
    width = values.shape[1]
    lane = lax.broadcasted_iota(jnp.int32, values.shape, 1)
    return jnp.where(lane == width - 1, 0.0, pltpu.roll(values, width - 1, 1))


def spread(values):
    wide = values.astype(F32)
    return jnp.concatenate(
        [shift_down(wide).astype(BF16), values, shift_up(wide).astype(BF16)], axis=0
    )


def combine(products):
    chans = products.shape[0] // 3
    return (
        products[chans : 2 * chans]
        + shift_up(products[:chans])
        + shift_down(products[2 * chans :])
    )


def planes_of(where):
    return (1, 2 * (1 - where[0]), 2 * where[0])


def fill(where, stack, inside, edges, field):
    rows = field.shape[0] - 2
    row = where[1]
    for plane in range(3):
        for r in range(rows):
            field[1 + r, plane] = stack[plane, r]
        field[(1 - row) * (rows + 1), plane] = inside[plane]
        field[row * (rows + 1), plane] = edges[plane]


def halves(where, quarter):
    mine = where[1]
    return [pl.ds(pl.multiple_of(2 * h * quarter + mine * quarter, quarter), quarter) for h in range(2)]


def fill_pair(where, stack, pair, edges, pair_edges, field, split):
    rows = (field.shape[0] - 2) // 2
    row = where[1]

    def put(at, plane, value):
        if not split:
            field[at, plane] = value[...]
            return
        quarter = field.shape[2] // 2
        for h, part in enumerate(halves(where, quarter)):
            field[at, plane, h * quarter : (h + 1) * quarter] = value[part]

    for plane in range(3):
        for r in range(rows):
            put(1 + row * rows + r, plane, stack.at[plane, r])
            put(1 + (1 - row) * rows + r, plane, pair(plane, r))
        put(row * (2 * rows + 1), plane, edges.at[plane])
        put((1 - row) * (2 * rows + 1), plane, pair_edges.at[plane])


def window(field, row):
    block = field[row : row + 3]
    return block.reshape(-1, block.shape[-1])


def conv_rows(weights, field, row):
    return combine(jnp.dot(weights[...], window(field, row), preferred_element_type=F32))


def gather_kernel(where, own, even, odd, *refs):
    stack, across, inside = refs
    for plane, slab in zip(planes_of(where), (own, even, odd)):
        stack[plane] = jnp.transpose(slab[:, 0], (1, 0, 2))
        across[plane] = stack[plane, where[1] * (stack.shape[1] - 1)]
        inside[plane] = stack[plane, (1 - where[1]) * (stack.shape[1] - 1)]


def gather_hidden_kernel(where, own, even, odd, stack, across, inside):
    last = own.shape[0] - 1
    for plane, slab in zip(planes_of(where), (own, even, odd)):
        stack[plane] = slab[...]
        across[plane] = slab[where[1] * last]
        inside[plane] = slab[(1 - where[1]) * last]


def weights_kernel(first, second, first_out, second_out, back_out):
    chans = first.shape[1]
    for b in range(3):
        for a in range(3):
            for e in range(3):
                tap = a * 9 + b * 3 + e
                at = (
                    slice(e * chans, (e + 1) * chans),
                    slice((b * 3 + a) * chans, (b * 3 + a + 1) * chans),
                )
                first_out[at] = first[tap]
                second_out[at] = second[tap]
                back_out[at] = second[26 - tap].T


def first_kernel(where, *refs):
    stack, inside, edges, weights, hidden, slope, shared, field = refs
    fill(where, stack, inside, edges, field)
    rows = hidden.shape[0]
    for plane in range(3):
        shared[plane * rows : (plane + 1) * rows] = stack[plane]
    shared[3 * rows : 3 * rows + 3] = edges[...]
    for row in range(hidden.shape[0]):
        value = conv_rows(weights, field, row)
        gate = 1.0 / (1.0 + jnp.exp(-value))
        hidden[row] = (value * gate).astype(BF16)
        shared[3 * rows + 3 + row] = hidden[row]
        slope[row] = gate * (1.0 + value * (1.0 - gate))


def second_kernel(where, *refs):
    stack, inside, edges, weights, out, field, held = refs
    fill(where, stack, inside, edges, field)
    for row in range(held.shape[0]):
        held[row] = conv_rows(weights, field, row).astype(BF16)
    out[:, 0] = jnp.transpose(held[...], (1, 0, 2))


def grad_kernel(where, *refs):
    weights, slope, keep, *rest = refs[3:]
    *send, field, whole = rest
    fill(where, *refs[:3], field)
    for row in range(slope.shape[0]):
        grad = (conv_rows(weights, field, row) * slope[row]).astype(BF16)
        if not send:
            keep[row] = grad
        else:
            whole[...] = grad
            quarter = keep.shape[1] // 2
            for h in range(2):
                at = pl.ds(h * quarter, quarter)
                mine = pl.ds(pl.multiple_of((2 * h + where[1]) * quarter, quarter), quarter)
                theirs = pl.ds(pl.multiple_of((2 * h + 1 - where[1]) * quarter, quarter), quarter)
                keep[row, at] = whole[mine]
                send[0][row, at] = whole[theirs]


def pair_off(where, total, send, keep):
    width = send.shape[1]
    mine = pl.multiple_of(where[2] * width, width)
    theirs = pl.multiple_of((1 - where[2]) * width, width)
    send[...] = total[:, pl.ds(theirs, width)].astype(BF16)
    keep[...] = total[:, pl.ds(mine, width)]


def ordered(where, own, pair, both):
    rows = own.shape[0]
    for r in range(rows):
        both[where[1] * rows + r] = own[r]
        both[(1 - where[1]) * rows + r] = pair[r]


def second_grad_kernel(where, *refs):
    stack, pair, edges, pair_edges, hidden, pair_shared, send, keep, field, both, total = refs
    rows = hidden.shape[0]
    fill_pair(where, stack, lambda p, r: pair.at[p, r], edges, pair_edges, field, True)
    ordered(where, hidden, pair_shared.at[pl.ds(3 * rows + 3, rows)], both)
    for row in range(both.shape[0]):
        part = lax.dot_general(
            window(field, row),
            spread(both[row]),
            (((1,), (1,)), ((), ())),
            preferred_element_type=F32,
        ).reshape(total.shape)
        total[...] = part if row == 0 else total[...] + part
    pair_off(where, total, send, keep)


def first_grad_kernel(where, *refs):
    stack, edges, pair_shared, grad, pair_grad, send, keep, field, both, total = refs
    rows = grad.shape[0]
    pair_edges = pair_shared.at[pl.ds(3 * rows, 3)]
    fill_pair(
        where, stack, lambda p, r: pair_shared.at[p * rows + r], edges, pair_edges, field, False
    )
    ordered(where, grad, pair_grad, both)
    for row in range(both.shape[0]):
        part = lax.dot_general(
            spread(both[row]),
            window(field, row),
            (((1,), (1,)), ((), ())),
            preferred_element_type=F32,
        ).reshape(total.shape)
        total[...] = part if row == 0 else total[...] + part
    pair_off(where, total, send, keep)


def second_total_kernel(where, *refs):
    hidden, total, field = refs[3:]
    fill(where, *refs[:3], field)
    for row in range(hidden.shape[0]):
        part = lax.dot_general(
            window(field, row),
            spread(hidden[row]),
            (((1,), (1,)), ((), ())),
            preferred_element_type=F32,
        ).reshape(total.shape)
        total[...] = part if row == 0 else total[...] + part


def first_total_kernel(where, *refs):
    grad, total, field = refs[3:]
    fill(where, *refs[:3], field)
    for row in range(grad.shape[0]):
        part = lax.dot_general(
            spread(grad[row]),
            window(field, row),
            (((1,), (1,)), ((), ())),
            preferred_element_type=F32,
        ).reshape(total.shape)
        total[...] = part if row == 0 else total[...] + part


def pack_kernel(where, held, arrived, *refs):
    sends = refs[:-2]
    keep, packed = refs[-2:]
    parts, tiles, outs, lanes = packed.shape
    group = lanes // parts
    per = held.shape[2] // lanes
    sums = {}
    for n in range(held.shape[0] * per):
        at = (n // per, slice(None), slice(n % per * lanes, (n % per + 1) * lanes))
        sums[n] = held[at] + arrived[at].astype(F32)
    lane = lax.broadcasted_iota(jnp.int32, (outs, lanes), 1) // group
    for tile in range(tiles):
        for part in range(parts):
            value = jnp.zeros((outs, lanes), F32)
            for place in range(parts):
                n = tile * parts + place
                if n in sums:
                    turned = sums[n]
                    if place != part:
                        turned = pltpu.roll(turned, (place - part) % parts * group, 1)
                    value = jnp.where(lane == place, turned, value)
            packed[part, tile] = value
    mine = where[3]
    keep[...] = packed[mine]
    for k, send in enumerate(sends):
        send[...] = packed[mine ^ (k + 1)].astype(BF16)


def finish_kernel(tap_of, factor, held, *refs):
    out = refs[-1]
    tiles, outs, lanes = held.shape
    group = out.shape[2]
    places = lanes // group
    for tile in range(tiles):
        total = held[tile]
        for arrived in refs[:-1]:
            total = total + arrived[tile].astype(F32)
        total = total * factor
        for place in range(places):
            n = tile * places + place
            if n < len(tap_of):
                out[tap_of[n]] = total[:, place * group : (place + 1) * group]


def struct(shape, dtype):
    return jax.ShapeDtypeStruct(shape, dtype)


def call(kernel, name, out_shapes, args, scratch=(), flops=0, scalars=True, busy=1):
    moved = sum(math.prod(a.shape) * a.dtype.itemsize for a in (*args, *out_shapes))
    return pl.pallas_call(
        kernel,
        name=name,
        in_specs=[SMEM] * scalars + [VMEM] * (len(args) - scalars),
        out_specs=[VMEM] * len(out_shapes),
        out_shape=out_shapes,
        scratch_shapes=[pltpu.VMEM(s.shape, s.dtype) for s in scratch],
        cost_estimate=pl.CostEstimate(
            flops=flops * busy, bytes_accessed=moved * busy, transcendentals=0
        ),
        compiler_params=pltpu.CompilerParams(vmem_limit_bytes=LIMIT),
    )(*args)


def after(value, *others):
    return lax.optimization_barrier((value, *others))[0]


def packed_parts(where, keep, arrived):
    taps, outs, width = keep.shape
    parts = lax.axis_size("cin")
    lanes = 128
    tiles = -(-taps * width // (lanes * parts))
    piece = (tiles, outs, lanes)
    return call(
        pack_kernel,
        "pack_parts",
        [struct(piece, BF16)] * (parts - 1) + [struct(piece, F32)],
        (where, keep, arrived),
        [struct((parts, *piece), F32)],
    )


def exchanged(sends):
    parts = lax.axis_size("cin")
    return [
        lax.ppermute(value, "cin", [(i, i ^ (k + 1)) for i in range(parts)])
        for k, value in enumerate(sends)
    ]


def finished(keep, arrived, tap_of, factor, shape):
    (total,) = call(
        functools.partial(finish_kernel, tap_of, factor),
        "finish_sum",
        [struct((shape[1], shape[0], shape[2]), F32)],
        (keep, *arrived),
        scalars=False,
    )
    return total.transpose(1, 0, 2)


def cross(values):
    return lax.ppermute(values, "cout", [(i, i ^ 2) for i in range(lax.axis_size("cout"))])


def scattered(grads, factor):
    part = lax.psum_scatter(grads, "cin", scatter_dimension=2, tiled=True)
    return lax.psum_scatter(part, "cout", scatter_dimension=0, tiled=True) * factor


def body(volume, first_filter, second_filter, cotangent):
    chans, planes, rows, width = volume.shape
    outs, taps, ins = second_filter.shape
    assert planes == 1 and outs == chans == ins
    plane_count = lax.axis_size("cin")
    row_count = lax.axis_size("cout")
    factor = 1.0 / math.sqrt(plane_count * planes * row_count * rows * width)
    plane_at = lax.axis_index("cin")
    row_at = lax.axis_index("cout")
    where = jnp.stack([plane_at % 2, row_at % 2, row_at // 2, plane_at]).astype(jnp.int32)
    pairwise = plane_count == 4 and row_count == 4
    flops = 2 * 27 * chans * chans * rows * width
    slab = struct((rows, chans, width), BF16)
    field = struct((rows + 2, 3, chans, width), BF16)
    matrix = struct((3 * chans, 9 * chans), BF16)

    stack = struct((3, rows, chans, width), BF16)
    edge = struct((3, chans, width), BF16)

    volume_planes = (swap_planes(volume, 0), swap_planes(volume, 1))
    grad_planes = (swap_planes(cotangent, 0), swap_planes(cotangent, 1))
    first_weights, second_weights, back_weights = call(
        weights_kernel,
        "weights",
        [matrix] * 3,
        (first_filter.transpose(1, 0, 2), second_filter.transpose(1, 0, 2)),
        scalars=False,
    )
    own, across, inside = call(
        gather_kernel,
        "gather_volume",
        [stack, edge, edge],
        (where, volume, after(volume_planes[0], first_weights), volume_planes[1]),
    )
    slabs = (own, swap_rows(inside, 0), swap_rows(across, 1))
    own, across, inside = call(
        gather_kernel,
        "gather_cotangent",
        [stack, edge, edge],
        (where, cotangent, *grad_planes),
    )
    grad_slabs = (own, swap_rows(inside, 0), swap_rows(across, 1))
    hidden, slope, shared = call(
        first_kernel,
        "first_conv",
        [slab, struct(slab.shape, F32), struct((4 * rows + 3, chans, width), BF16)],
        (where, *slabs, first_weights),
        [field],
        flops,
        busy=1,
    )
    pair_shared = swap_rows(shared, 0)
    hidden_even, hidden_odd = swap_planes(hidden, 0), swap_planes(hidden, 1)
    half = struct((rows, chans // 2, width), BF16)
    grads = call(
        grad_kernel,
        "hidden_grad",
        [half, half] if pairwise else [slab],
        (where, *grad_slabs, back_weights, slope),
        [field, struct((chans, width), BF16)],
        flops,
        busy=20,
    )
    shape = (outs // row_count, taps, ins // plane_count)

    def hidden_rows(even, odd):
        own, across, inside = call(
            gather_hidden_kernel, "gather_hidden", [stack, edge, edge], (where, hidden, even, odd)
        )
        return own, swap_rows(inside, 0), swap_rows(across, 1)

    def convolved(*slabs):
        (out,) = call(
            second_kernel,
            "second_conv",
            [struct(volume.shape, BF16)],
            (where, *slabs, second_weights),
            [field, slab],
            flops,
        )
        return out

    if pairwise:
        wide = 2 * rows + 2
        block = shape[0]
        second_send, second_keep = call(
            second_grad_kernel,
            "second_filter_grad",
            [struct((9, block, 3 * ins), BF16), struct((9, block, 3 * ins), F32)],
            (
                where,
                grad_slabs[0],
                swap_rows(after(grad_slabs[0], hidden), 0),
                grad_slabs[2],
                swap_rows(grad_slabs[2], 0),
                hidden,
                pair_shared,
            ),
            [
                struct((wide, 3, 2 * block, width), BF16),
                struct((2 * rows, chans, width), BF16),
                struct((9, 2 * block, 3 * ins), F32),
            ],
            flops,
            busy=0,
        )
        second_arrived = cross(second_send)
        first_send, first_keep = call(
            first_grad_kernel,
            "first_filter_grad",
            [struct((3, block, 9 * ins), BF16), struct((3, block, 9 * ins), F32)],
            (
                where,
                slabs[0],
                slabs[2],
                pair_shared,
                after(grads[0], second_send),
                swap_rows(grads[1], 0),
            ),
            [
                struct((wide, 3, chans, width), BF16),
                struct((2 * rows, 2 * block, width), BF16),
                struct((3, 2 * block, 9 * ins), F32),
            ],
            flops,
            busy=0,
        )
        first_arrived = cross(first_send)
        hidden_slabs = hidden_rows(after(hidden_even, first_send), hidden_odd)
        steps = range(3)
        second_taps = [26 - (a * 9 + b * 3 + e) for b in steps for a in steps for e in steps]
        first_taps = [a * 9 + b * 3 + e for e in steps for b in steps for a in steps]
        *second_parts, second_keep = packed_parts(
            where, after(second_keep, hidden_slabs[1]), second_arrived
        )
        second_parts = exchanged(second_parts)
        *first_parts, first_keep = packed_parts(
            where, after(first_keep, second_keep), first_arrived
        )
        first_parts = exchanged(first_parts)
        second_sum = finished(
            after(second_keep, first_keep), second_parts, second_taps, factor, shape
        )
        second_out = convolved(after(hidden_slabs[0], second_sum), *hidden_slabs[1:])
        first_sum = finished(
            after(first_keep, second_out), first_parts, first_taps, factor, shape
        )
    else:
        second_out = convolved(*hidden_rows(hidden_even, hidden_odd))
        (second_total,) = call(
            second_total_kernel,
            "second_filter_grad",
            [struct((9, outs, 3 * ins), F32)],
            (where, *grad_slabs, hidden),
            [field],
            flops,
        )
        (first_total,) = call(
            first_total_kernel,
            "first_filter_grad",
            [struct((3, outs, 9 * ins), F32)],
            (where, *slabs, *grads),
            [field],
            flops,
        )
        second_total = second_total.reshape(3, 3, outs, 3, ins).transpose(2, 1, 0, 3, 4)
        second_total = jnp.flip(second_total, axis=(1, 2, 3)).reshape(outs, taps, ins)
        first_total = first_total.reshape(3, outs, 3, 3, ins).transpose(1, 3, 2, 0, 4)
        second_sum = scattered(second_total, factor)
        first_sum = scattered(first_total.reshape(outs, taps, ins), factor)
    return (second_out, first_sum, second_sum)


def solution(mesh):
    return jax.shard_map(
        body,
        mesh=mesh,
        in_specs=(
            P(None, ("grp", "cin"), "cout", None),
            P(),
            P(),
            P(None, ("grp", "cin"), "cout", None),
        ),
        out_specs=(
            P(None, ("grp", "cin"), "cout", None),
            P("cout", "grp", "cin"),
            P("cout", "grp", "cin"),
        ),
        check_vma=False,
    )
```

```python
import functools
import math

import jax
import jax.numpy as jnp
from jax import lax
from jax.experimental import pallas as pl
from jax.experimental.pallas import tpu as pltpu
from jax.sharding import PartitionSpec as P

VMEM = pl.BlockSpec(memory_space=pltpu.VMEM)
SMEM = pl.BlockSpec(memory_space=pltpu.SMEM)
F32 = jnp.float32
BF16 = jnp.bfloat16
LIMIT = 14 * 1024 * 1024


def links(count, odd):
    pairs = []
    for i in range(odd, count - 1, 2):
        pairs += [(i, i + 1), (i + 1, i)]
    return pairs


def swap_planes(values, odd):
    return lax.ppermute(values, "cin", links(lax.axis_size("cin"), odd))


def swap_rows(values, odd):
    return lax.ppermute(values, "cout", links(lax.axis_size("cout"), odd))


def shift_up(values):
    lane = lax.broadcasted_iota(jnp.int32, values.shape, 1)
    return jnp.where(lane == 0, 0.0, pltpu.roll(values, 1, 1))


def shift_down(values):
    width = values.shape[1]
    lane = lax.broadcasted_iota(jnp.int32, values.shape, 1)
    return jnp.where(lane == width - 1, 0.0, pltpu.roll(values, width - 1, 1))


def spread(values):
    wide = values.astype(F32)
    return jnp.concatenate(
        [shift_down(wide).astype(BF16), values, shift_up(wide).astype(BF16)], axis=0
    )


def combine(products):
    chans = products.shape[0] // 3
    return (
        products[chans : 2 * chans]
        + shift_up(products[:chans])
        + shift_down(products[2 * chans :])
    )


def planes_of(where):
    return (1, 2 * where[0], 2 * (1 - where[0]))


def fill(where, stack, inside, edges, field):
    rows = field.shape[0] - 2
    row = where[1]
    for plane in range(3):
        for r in range(rows):
            field[1 + r, plane] = stack[plane, r]
        field[(1 - row) * (rows + 1), plane] = inside[plane]
        field[row * (rows + 1), plane] = edges[plane]


def halves(where, quarter):
    mine = where[1]
    return [pl.ds(pl.multiple_of(2 * h * quarter + mine * quarter, quarter), quarter) for h in range(2)]


def fill_pair(where, stack, pair, edges, pair_edges, field, split):
    rows = (field.shape[0] - 2) // 2
    row = where[1]

    def put(at, plane, value):
        if not split:
            field[at, plane] = value[...]
            return
        quarter = field.shape[2] // 2
        for h, part in enumerate(halves(where, quarter)):
            field[at, plane, h * quarter : (h + 1) * quarter] = value[part]

    for plane in range(3):
        for r in range(rows):
            put(1 + row * rows + r, plane, stack.at[plane, r])
            put(1 + (1 - row) * rows + r, plane, pair(plane, r))
        put(row * (2 * rows + 1), plane, edges.at[plane])
        put((1 - row) * (2 * rows + 1), plane, pair_edges.at[plane])


def window(field, row):
    block = field[row : row + 3]
    return block.reshape(-1, block.shape[-1])


def conv_rows(weights, field, row):
    return combine(jnp.dot(weights[...], window(field, row), preferred_element_type=F32))


def gather_kernel(where, own, odd, even, *refs):
    stack, across, inside = refs
    for plane, slab in zip(planes_of(where), (own, odd, even)):
        stack[plane] = jnp.transpose(slab[:, 0], (1, 0, 2))
        across[plane] = stack[plane, where[1] * (stack.shape[1] - 1)]
        inside[plane] = stack[plane, (1 - where[1]) * (stack.shape[1] - 1)]


def gather_hidden_kernel(where, own, odd, even, stack, across, inside):
    last = own.shape[0] - 1
    for plane, slab in zip(planes_of(where), (own, odd, even)):
        stack[plane] = slab[...]
        across[plane] = slab[where[1] * last]
        inside[plane] = slab[(1 - where[1]) * last]


def weights_kernel(first, second, first_out, second_out, back_out):
    chans = first.shape[1]
    for b in range(3):
        for a in range(3):
            for e in range(3):
                tap = a * 9 + b * 3 + e
                at = (
                    slice(e * chans, (e + 1) * chans),
                    slice((b * 3 + a) * chans, (b * 3 + a + 1) * chans),
                )
                first_out[at] = first[tap]
                second_out[at] = second[tap]
                back_out[at] = second[26 - tap].T


def first_kernel(where, *refs):
    stack, inside, edges, weights, hidden, slope, shared, field = refs
    fill(where, stack, inside, edges, field)
    rows = hidden.shape[0]
    for plane in range(3):
        shared[plane * rows : (plane + 1) * rows] = stack[plane]
    shared[3 * rows : 3 * rows + 3] = edges[...]
    for row in range(hidden.shape[0]):
        value = conv_rows(weights, field, row)
        gate = 1.0 / (1.0 + jnp.exp(-value))
        hidden[row] = (value * gate).astype(BF16)
        shared[3 * rows + 3 + row] = hidden[row]
        slope[row] = gate * (1.0 + value * (1.0 - gate))


def second_kernel(where, *refs):
    stack, inside, edges, weights, out, field, held = refs
    fill(where, stack, inside, edges, field)
    for row in range(held.shape[0]):
        held[row] = conv_rows(weights, field, row).astype(BF16)
    out[:, 0] = jnp.transpose(held[...], (1, 0, 2))


def grad_kernel(where, *refs):
    weights, slope, keep, *rest = refs[3:]
    *send, field, whole = rest
    fill(where, *refs[:3], field)
    for row in range(slope.shape[0]):
        grad = (conv_rows(weights, field, row) * slope[row]).astype(BF16)
        if not send:
            keep[row] = grad
        else:
            whole[...] = grad
            quarter = keep.shape[1] // 2
            for h in range(2):
                at = pl.ds(h * quarter, quarter)
                mine = pl.ds(pl.multiple_of((2 * h + where[1]) * quarter, quarter), quarter)
                theirs = pl.ds(pl.multiple_of((2 * h + 1 - where[1]) * quarter, quarter), quarter)
                keep[row, at] = whole[mine]
                send[0][row, at] = whole[theirs]


def pair_off(where, total, send, keep):
    width = send.shape[1]
    mine = pl.multiple_of(where[2] * width, width)
    theirs = pl.multiple_of((1 - where[2]) * width, width)
    send[...] = total[:, pl.ds(theirs, width)].astype(BF16)
    keep[...] = total[:, pl.ds(mine, width)]


def ordered(where, own, pair, both):
    rows = own.shape[0]
    for r in range(rows):
        both[where[1] * rows + r] = own[r]
        both[(1 - where[1]) * rows + r] = pair[r]


def second_grad_kernel(where, *refs):
    stack, pair, edges, pair_edges, hidden, pair_shared, send, keep, field, both, total = refs
    rows = hidden.shape[0]
    fill_pair(where, stack, lambda p, r: pair.at[p, r], edges, pair_edges, field, True)
    ordered(where, hidden, pair_shared.at[pl.ds(3 * rows + 3, rows)], both)
    for row in range(both.shape[0]):
        part = lax.dot_general(
            window(field, row),
            spread(both[row]),
            (((1,), (1,)), ((), ())),
            preferred_element_type=F32,
        ).reshape(total.shape)
        total[...] = part if row == 0 else total[...] + part
    pair_off(where, total, send, keep)


def first_grad_kernel(where, *refs):
    stack, edges, pair_shared, grad, pair_grad, send, keep, field, both, total = refs
    rows = grad.shape[0]
    pair_edges = pair_shared.at[pl.ds(3 * rows, 3)]
    fill_pair(
        where, stack, lambda p, r: pair_shared.at[p * rows + r], edges, pair_edges, field, False
    )
    ordered(where, grad, pair_grad, both)
    for row in range(both.shape[0]):
        part = lax.dot_general(
            spread(both[row]),
            window(field, row),
            (((1,), (1,)), ((), ())),
            preferred_element_type=F32,
        ).reshape(total.shape)
        total[...] = part if row == 0 else total[...] + part
    pair_off(where, total, send, keep)


def second_total_kernel(where, *refs):
    hidden, total, field = refs[3:]
    fill(where, *refs[:3], field)
    for row in range(hidden.shape[0]):
        part = lax.dot_general(
            window(field, row),
            spread(hidden[row]),
            (((1,), (1,)), ((), ())),
            preferred_element_type=F32,
        ).reshape(total.shape)
        total[...] = part if row == 0 else total[...] + part


def first_total_kernel(where, *refs):
    grad, total, field = refs[3:]
    fill(where, *refs[:3], field)
    for row in range(grad.shape[0]):
        part = lax.dot_general(
            spread(grad[row]),
            window(field, row),
            (((1,), (1,)), ((), ())),
            preferred_element_type=F32,
        ).reshape(total.shape)
        total[...] = part if row == 0 else total[...] + part


def pack_kernel(where, held, arrived, *refs):
    sends = refs[:-2]
    keep, packed = refs[-2:]
    parts, tiles, outs, lanes = packed.shape
    group = lanes // parts
    per = held.shape[2] // lanes
    sums = {}
    for n in range(held.shape[0] * per):
        at = (n // per, slice(None), slice(n % per * lanes, (n % per + 1) * lanes))
        sums[n] = held[at] + arrived[at].astype(F32)
    lane = lax.broadcasted_iota(jnp.int32, (outs, lanes), 1) // group
    for tile in range(tiles):
        for part in range(parts):
            value = jnp.zeros((outs, lanes), F32)
            for place in range(parts):
                n = tile * parts + place
                if n in sums:
                    turned = sums[n]
                    if place != part:
                        turned = pltpu.roll(turned, (place - part) % parts * group, 1)
                    value = jnp.where(lane == place, turned, value)
            packed[part, tile] = value
    mine = where[3]
    keep[...] = packed[mine]
    for k, send in enumerate(sends):
        send[...] = packed[mine ^ (k + 1)].astype(BF16)


def finish_kernel(tap_of, factor, held, *refs):
    out = refs[-1]
    tiles, outs, lanes = held.shape
    group = out.shape[2]
    places = lanes // group
    for tile in range(tiles):
        total = held[tile]
        for arrived in refs[:-1]:
            total = total + arrived[tile].astype(F32)
        total = total * factor
        for place in range(places):
            n = tile * places + place
            if n < len(tap_of):
                out[tap_of[n]] = total[:, place * group : (place + 1) * group]


def struct(shape, dtype):
    return jax.ShapeDtypeStruct(shape, dtype)


def call(kernel, name, out_shapes, args, scratch=(), flops=0, scalars=True, busy=1):
    moved = sum(math.prod(a.shape) * a.dtype.itemsize for a in (*args, *out_shapes))
    return pl.pallas_call(
        kernel,
        name=name,
        in_specs=[SMEM] * scalars + [VMEM] * (len(args) - scalars),
        out_specs=[VMEM] * len(out_shapes),
        out_shape=out_shapes,
        scratch_shapes=[pltpu.VMEM(s.shape, s.dtype) for s in scratch],
        cost_estimate=pl.CostEstimate(
            flops=flops * busy, bytes_accessed=moved * busy, transcendentals=0
        ),
        compiler_params=pltpu.CompilerParams(vmem_limit_bytes=LIMIT),
    )(*args)


def after(value, *others):
    return lax.optimization_barrier((value, *others))[0]


def packed_parts(where, keep, arrived):
    taps, outs, width = keep.shape
    parts = lax.axis_size("cin")
    lanes = 128
    tiles = -(-taps * width // (lanes * parts))
    piece = (tiles, outs, lanes)
    return call(
        pack_kernel,
        "pack_parts",
        [struct(piece, BF16)] * (parts - 1) + [struct(piece, F32)],
        (where, keep, arrived),
        [struct((parts, *piece), F32)],
    )


def exchanged(sends):
    parts = lax.axis_size("cin")
    return [
        lax.ppermute(value, "cin", [(i, i ^ (k + 1)) for i in range(parts)])
        for k, value in reversed(list(enumerate(sends)))
    ]


def finished(keep, arrived, tap_of, factor, shape):
    (total,) = call(
        functools.partial(finish_kernel, tap_of, factor),
        "finish_sum",
        [struct((shape[1], shape[0], shape[2]), F32)],
        (keep, *arrived),
        scalars=False,
    )
    return total.transpose(1, 0, 2)


def cross(values):
    return lax.ppermute(values, "cout", [(i, i ^ 2) for i in range(lax.axis_size("cout"))])


def scattered(grads, factor):
    part = lax.psum_scatter(grads, "cin", scatter_dimension=2, tiled=True)
    return lax.psum_scatter(part, "cout", scatter_dimension=0, tiled=True) * factor


def body(volume, first_filter, second_filter, cotangent):
    chans, planes, rows, width = volume.shape
    outs, taps, ins = second_filter.shape
    assert planes == 1 and outs == chans == ins
    plane_count = lax.axis_size("cin")
    row_count = lax.axis_size("cout")
    factor = 1.0 / math.sqrt(plane_count * planes * row_count * rows * width)
    plane_at = lax.axis_index("cin")
    row_at = lax.axis_index("cout")
    where = jnp.stack([plane_at % 2, row_at % 2, row_at // 2, plane_at]).astype(jnp.int32)
    pairwise = plane_count == 4 and row_count == 4
    flops = 2 * 27 * chans * chans * rows * width
    slab = struct((rows, chans, width), BF16)
    field = struct((rows + 2, 3, chans, width), BF16)
    matrix = struct((3 * chans, 9 * chans), BF16)

    stack = struct((3, rows, chans, width), BF16)
    edge = struct((3, chans, width), BF16)

    volume_planes = (swap_planes(volume, 1), swap_planes(volume, 0))
    grad_planes = (swap_planes(cotangent, 1), swap_planes(cotangent, 0))
    first_weights, second_weights, back_weights = call(
        weights_kernel,
        "weights",
        [matrix] * 3,
        (first_filter.transpose(1, 0, 2), second_filter.transpose(1, 0, 2)),
        scalars=False,
    )
    own, across, inside = call(
        gather_kernel,
        "gather_volume",
        [stack, edge, edge],
        (where, volume, after(volume_planes[0], first_weights), volume_planes[1]),
    )
    slabs = (own, swap_rows(inside, 0), swap_rows(across, 1))
    own, across, inside = call(
        gather_kernel,
        "gather_cotangent",
        [stack, edge, edge],
        (where, cotangent, *grad_planes),
    )
    grad_slabs = (own, swap_rows(inside, 0), swap_rows(across, 1))
    hidden, slope, shared = call(
        first_kernel,
        "first_conv",
        [slab, struct(slab.shape, F32), struct((4 * rows + 3, chans, width), BF16)],
        (where, *slabs, first_weights),
        [field],
        flops,
        busy=1,
    )
    pair_shared = swap_rows(shared, 0)
    hidden_odd, hidden_even = swap_planes(hidden, 1), swap_planes(hidden, 0)
    half = struct((rows, chans // 2, width), BF16)
    grads = call(
        grad_kernel,
        "hidden_grad",
        [half, half] if pairwise else [slab],
        (where, *grad_slabs, back_weights, slope),
        [field, struct((chans, width), BF16)],
        flops,
        busy=20,
    )
    shape = (outs // row_count, taps, ins // plane_count)

    def hidden_rows(odd, even):
        own, across, inside = call(
            gather_hidden_kernel, "gather_hidden", [stack, edge, edge], (where, hidden, odd, even)
        )
        return own, swap_rows(inside, 0), swap_rows(across, 1)

    def convolved(*slabs):
        (out,) = call(
            second_kernel,
            "second_conv",
            [struct(volume.shape, BF16)],
            (where, *slabs, second_weights),
            [field, slab],
            flops,
        )
        return out

    if pairwise:
        wide = 2 * rows + 2
        block = shape[0]
        second_send, second_keep = call(
            second_grad_kernel,
            "second_filter_grad",
            [struct((9, block, 3 * ins), BF16), struct((9, block, 3 * ins), F32)],
            (
                where,
                grad_slabs[0],
                swap_rows(grad_slabs[0], 0),
                grad_slabs[2],
                swap_rows(grad_slabs[2], 0),
                hidden,
                pair_shared,
            ),
            [
                struct((wide, 3, 2 * block, width), BF16),
                struct((2 * rows, chans, width), BF16),
                struct((9, 2 * block, 3 * ins), F32),
            ],
            flops,
            busy=0,
        )
        second_arrived = cross(second_send)
        first_send, first_keep = call(
            first_grad_kernel,
            "first_filter_grad",
            [struct((3, block, 9 * ins), BF16), struct((3, block, 9 * ins), F32)],
            (
                where,
                slabs[0],
                slabs[2],
                pair_shared,
                after(grads[0], second_send),
                swap_rows(grads[1], 0),
            ),
            [
                struct((wide, 3, chans, width), BF16),
                struct((2 * rows, 2 * block, width), BF16),
                struct((3, 2 * block, 9 * ins), F32),
            ],
            flops,
            busy=0,
        )
        first_arrived = cross(first_send)
        hidden_slabs = hidden_rows(after(hidden_odd, first_send), hidden_even)
        steps = range(3)
        second_taps = [26 - (a * 9 + b * 3 + e) for b in steps for a in steps for e in steps]
        first_taps = [a * 9 + b * 3 + e for e in steps for b in steps for a in steps]
        *second_parts, second_keep = packed_parts(
            where, after(second_keep, hidden_slabs[1]), second_arrived
        )
        second_parts = exchanged(second_parts)
        *first_parts, first_keep = packed_parts(
            where, after(first_keep, second_keep), first_arrived
        )
        first_parts = exchanged(first_parts)
        second_sum = finished(
            after(second_keep, first_keep), second_parts, second_taps, factor, shape
        )
        second_out = convolved(after(hidden_slabs[0], second_sum), *hidden_slabs[1:])
        first_sum = finished(
            after(first_keep, second_out), first_parts, first_taps, factor, shape
        )
    else:
        second_out = convolved(*hidden_rows(hidden_odd, hidden_even))
        (second_total,) = call(
            second_total_kernel,
            "second_filter_grad",
            [struct((9, outs, 3 * ins), F32)],
            (where, *grad_slabs, hidden),
            [field],
            flops,
        )
        (first_total,) = call(
            first_total_kernel,
            "first_filter_grad",
            [struct((3, outs, 9 * ins), F32)],
            (where, *slabs, *grads),
            [field],
            flops,
        )
        second_total = second_total.reshape(3, 3, outs, 3, ins).transpose(2, 1, 0, 3, 4)
        second_total = jnp.flip(second_total, axis=(1, 2, 3)).reshape(outs, taps, ins)
        first_total = first_total.reshape(3, outs, 3, 3, ins).transpose(1, 3, 2, 0, 4)
        second_sum = scattered(second_total, factor)
        first_sum = scattered(first_total.reshape(outs, taps, ins), factor)
    return (second_out, first_sum, second_sum)


def solution(mesh):
    return jax.shard_map(
        body,
        mesh=mesh,
        in_specs=(
            P(None, ("grp", "cin"), "cout", None),
            P(),
            P(),
            P(None, ("grp", "cin"), "cout", None),
        ),
        out_specs=(
            P(None, ("grp", "cin"), "cout", None),
            P("cout", "grp", "cin"),
            P("cout", "grp", "cin"),
        ),
        check_vma=False,
    )
```

```python
import functools
import math

import jax
import jax.numpy as jnp
from jax import lax
from jax.experimental import pallas as pl
from jax.experimental.pallas import tpu as pltpu
from jax.sharding import PartitionSpec as P

VMEM = pl.BlockSpec(memory_space=pltpu.VMEM)
SMEM = pl.BlockSpec(memory_space=pltpu.SMEM)
F32 = jnp.float32
BF16 = jnp.bfloat16
LIMIT = 14 * 1024 * 1024


def links(count, odd):
    pairs = []
    for i in range(odd, count - 1, 2):
        pairs += [(i, i + 1), (i + 1, i)]
    return pairs


def swap_planes(values, odd):
    return lax.ppermute(values, "cin", links(lax.axis_size("cin"), odd))


def swap_rows(values, odd):
    return lax.ppermute(values, "cout", links(lax.axis_size("cout"), odd))


def shift_up(values):
    lane = lax.broadcasted_iota(jnp.int32, values.shape, 1)
    return jnp.where(lane == 0, 0.0, pltpu.roll(values, 1, 1))


def shift_down(values):
    width = values.shape[1]
    lane = lax.broadcasted_iota(jnp.int32, values.shape, 1)
    return jnp.where(lane == width - 1, 0.0, pltpu.roll(values, width - 1, 1))


def spread(values):
    wide = values.astype(F32)
    return jnp.concatenate(
        [shift_down(wide).astype(BF16), values, shift_up(wide).astype(BF16)], axis=0
    )


def combine(products):
    chans = products.shape[0] // 3
    return (
        products[chans : 2 * chans]
        + shift_up(products[:chans])
        + shift_down(products[2 * chans :])
    )


def planes_of(where):
    return (1, 2 * where[0], 2 * (1 - where[0]))


def fill(where, stack, inside, edges, field):
    rows = field.shape[0] - 2
    row = where[1]
    for plane in range(3):
        for r in range(rows):
            field[1 + r, plane] = stack[plane, r]
        field[(1 - row) * (rows + 1), plane] = inside[plane]
        field[row * (rows + 1), plane] = edges[plane]


def halves(where, quarter):
    mine = where[1]
    return [pl.ds(pl.multiple_of(2 * h * quarter + mine * quarter, quarter), quarter) for h in range(2)]


def fill_pair(where, stack, pair, edges, pair_edges, field, split):
    rows = (field.shape[0] - 2) // 2
    row = where[1]

    def put(at, plane, value):
        if not split:
            field[at, plane] = value[...]
            return
        quarter = field.shape[2] // 2
        for h, part in enumerate(halves(where, quarter)):
            field[at, plane, h * quarter : (h + 1) * quarter] = value[part]

    for plane in range(3):
        for r in range(rows):
            put(1 + row * rows + r, plane, stack.at[plane, r])
            put(1 + (1 - row) * rows + r, plane, pair(plane, r))
        put(row * (2 * rows + 1), plane, edges.at[plane])
        put((1 - row) * (2 * rows + 1), plane, pair_edges.at[plane])


def window(field, row):
    block = field[row : row + 3]
    return block.reshape(-1, block.shape[-1])


def conv_rows(weights, field, row):
    return combine(jnp.dot(weights[...], window(field, row), preferred_element_type=F32))


def gather_kernel(where, own, odd, even, *refs):
    stack, across, inside = refs
    for plane, slab in zip(planes_of(where), (own, odd, even)):
        stack[plane] = jnp.transpose(slab[:, 0], (1, 0, 2))
        across[plane] = stack[plane, where[1] * (stack.shape[1] - 1)]
        inside[plane] = stack[plane, (1 - where[1]) * (stack.shape[1] - 1)]


def gather_hidden_kernel(where, own, even, odd, stack, across, inside):
    last = own.shape[0] - 1
    for plane, slab in zip(planes_of(where), (own, odd, even)):
        stack[plane] = slab[...]
        across[plane] = slab[where[1] * last]
        inside[plane] = slab[(1 - where[1]) * last]


def weights_kernel(first, second, first_out, second_out, back_out):
    chans = first.shape[1]
    for b in range(3):
        for a in range(3):
            for e in range(3):
                tap = a * 9 + b * 3 + e
                at = (
                    slice(e * chans, (e + 1) * chans),
                    slice((b * 3 + a) * chans, (b * 3 + a + 1) * chans),
                )
                first_out[at] = first[tap]
                second_out[at] = second[tap]
                back_out[at] = second[26 - tap].T


def first_kernel(where, *refs):
    stack, inside, edges, weights, hidden, slope, shared, field = refs
    fill(where, stack, inside, edges, field)
    rows = hidden.shape[0]
    for plane in range(3):
        shared[plane * rows : (plane + 1) * rows] = stack[plane]
    shared[3 * rows : 3 * rows + 3] = edges[...]
    for row in range(hidden.shape[0]):
        value = conv_rows(weights, field, row)
        gate = 1.0 / (1.0 + jnp.exp(-value))
        hidden[row] = (value * gate).astype(BF16)
        shared[3 * rows + 3 + row] = hidden[row]
        slope[row] = gate * (1.0 + value * (1.0 - gate))


def second_kernel(where, *refs):
    stack, inside, edges, weights, out, field, held = refs
    fill(where, stack, inside, edges, field)
    for row in range(held.shape[0]):
        held[row] = conv_rows(weights, field, row).astype(BF16)
    out[:, 0] = jnp.transpose(held[...], (1, 0, 2))


def grad_kernel(where, *refs):
    weights, slope, keep, *rest = refs[3:]
    *send, field, whole = rest
    fill(where, *refs[:3], field)
    for row in range(slope.shape[0]):
        grad = (conv_rows(weights, field, row) * slope[row]).astype(BF16)
        if not send:
            keep[row] = grad
        else:
            whole[...] = grad
            quarter = keep.shape[1] // 2
            for h in range(2):
                at = pl.ds(h * quarter, quarter)
                mine = pl.ds(pl.multiple_of((2 * h + where[1]) * quarter, quarter), quarter)
                theirs = pl.ds(pl.multiple_of((2 * h + 1 - where[1]) * quarter, quarter), quarter)
                keep[row, at] = whole[mine]
                send[0][row, at] = whole[theirs]


def pair_off(where, total, send, keep):
    width = send.shape[1]
    mine = pl.multiple_of(where[2] * width, width)
    theirs = pl.multiple_of((1 - where[2]) * width, width)
    send[...] = total[:, pl.ds(theirs, width)].astype(BF16)
    keep[...] = total[:, pl.ds(mine, width)]


def ordered(where, own, pair, both):
    rows = own.shape[0]
    for r in range(rows):
        both[where[1] * rows + r] = own[r]
        both[(1 - where[1]) * rows + r] = pair[r]


def second_grad_kernel(where, *refs):
    stack, pair, edges, pair_edges, hidden, pair_shared, send, keep, field, both, total = refs
    rows = hidden.shape[0]
    fill_pair(where, stack, lambda p, r: pair.at[p, r], edges, pair_edges, field, True)
    ordered(where, hidden, pair_shared.at[pl.ds(3 * rows + 3, rows)], both)
    for row in range(both.shape[0]):
        part = lax.dot_general(
            window(field, row),
            spread(both[row]),
            (((1,), (1,)), ((), ())),
            preferred_element_type=F32,
        ).reshape(total.shape)
        total[...] = part if row == 0 else total[...] + part
    pair_off(where, total, send, keep)


def first_grad_kernel(where, *refs):
    stack, edges, pair_shared, grad, pair_grad, send, keep, field, both, total = refs
    rows = grad.shape[0]
    pair_edges = pair_shared.at[pl.ds(3 * rows, 3)]
    fill_pair(
        where, stack, lambda p, r: pair_shared.at[p * rows + r], edges, pair_edges, field, False
    )
    ordered(where, grad, pair_grad, both)
    for row in range(both.shape[0]):
        part = lax.dot_general(
            spread(both[row]),
            window(field, row),
            (((1,), (1,)), ((), ())),
            preferred_element_type=F32,
        ).reshape(total.shape)
        total[...] = part if row == 0 else total[...] + part
    pair_off(where, total, send, keep)


def second_total_kernel(where, *refs):
    hidden, total, field = refs[3:]
    fill(where, *refs[:3], field)
    for row in range(hidden.shape[0]):
        part = lax.dot_general(
            window(field, row),
            spread(hidden[row]),
            (((1,), (1,)), ((), ())),
            preferred_element_type=F32,
        ).reshape(total.shape)
        total[...] = part if row == 0 else total[...] + part


def first_total_kernel(where, *refs):
    grad, total, field = refs[3:]
    fill(where, *refs[:3], field)
    for row in range(grad.shape[0]):
        part = lax.dot_general(
            spread(grad[row]),
            window(field, row),
            (((1,), (1,)), ((), ())),
            preferred_element_type=F32,
        ).reshape(total.shape)
        total[...] = part if row == 0 else total[...] + part


def pack_kernel(where, held, arrived, *refs):
    sends = refs[:-2]
    keep, packed = refs[-2:]
    parts, tiles, outs, lanes = packed.shape
    group = lanes // parts
    per = held.shape[2] // lanes
    sums = {}
    for n in range(held.shape[0] * per):
        at = (n // per, slice(None), slice(n % per * lanes, (n % per + 1) * lanes))
        sums[n] = held[at] + arrived[at].astype(F32)
    lane = lax.broadcasted_iota(jnp.int32, (outs, lanes), 1) // group
    for tile in range(tiles):
        for part in range(parts):
            value = jnp.zeros((outs, lanes), F32)
            for place in range(parts):
                n = tile * parts + place
                if n in sums:
                    turned = sums[n]
                    if place != part:
                        turned = pltpu.roll(turned, (place - part) % parts * group, 1)
                    value = jnp.where(lane == place, turned, value)
            packed[part, tile] = value
    mine = where[3]
    keep[...] = packed[mine]
    for k, send in enumerate(sends):
        send[...] = packed[mine ^ (k + 1)].astype(BF16)


def finish_kernel(tap_of, factor, held, *refs):
    out = refs[-1]
    tiles, outs, lanes = held.shape
    group = out.shape[2]
    places = lanes // group
    for tile in range(tiles):
        total = held[tile]
        for arrived in refs[:-1]:
            total = total + arrived[tile].astype(F32)
        total = total * factor
        for place in range(places):
            n = tile * places + place
            if n < len(tap_of):
                out[tap_of[n]] = total[:, place * group : (place + 1) * group]


def struct(shape, dtype):
    return jax.ShapeDtypeStruct(shape, dtype)


def call(kernel, name, out_shapes, args, scratch=(), flops=0, scalars=True, busy=1):
    moved = sum(math.prod(a.shape) * a.dtype.itemsize for a in (*args, *out_shapes))
    return pl.pallas_call(
        kernel,
        name=name,
        in_specs=[SMEM] * scalars + [VMEM] * (len(args) - scalars),
        out_specs=[VMEM] * len(out_shapes),
        out_shape=out_shapes,
        scratch_shapes=[pltpu.VMEM(s.shape, s.dtype) for s in scratch],
        cost_estimate=pl.CostEstimate(
            flops=flops * busy, bytes_accessed=moved * busy, transcendentals=0
        ),
        compiler_params=pltpu.CompilerParams(vmem_limit_bytes=LIMIT),
    )(*args)


def after(value, *others):
    return lax.optimization_barrier((value, *others))[0]


def packed_parts(where, keep, arrived):
    taps, outs, width = keep.shape
    parts = lax.axis_size("cin")
    lanes = 128
    tiles = -(-taps * width // (lanes * parts))
    piece = (tiles, outs, lanes)
    return call(
        pack_kernel,
        "pack_parts",
        [struct(piece, BF16)] * (parts - 1) + [struct(piece, F32)],
        (where, keep, arrived),
        [struct((parts, *piece), F32)],
    )


def exchanged(sends):
    parts = lax.axis_size("cin")
    return [
        lax.ppermute(value, "cin", [(i, i ^ (k + 1)) for i in range(parts)])
        for k, value in [(k, sends[k]) for k in (2, 0, 1)]
    ]


def finished(keep, arrived, tap_of, factor, shape):
    (total,) = call(
        functools.partial(finish_kernel, tap_of, factor),
        "finish_sum",
        [struct((shape[1], shape[0], shape[2]), F32)],
        (keep, *arrived),
        scalars=False,
    )
    return total.transpose(1, 0, 2)


def cross(values):
    return lax.ppermute(values, "cout", [(i, i ^ 2) for i in range(lax.axis_size("cout"))])


def scattered(grads, factor):
    part = lax.psum_scatter(grads, "cin", scatter_dimension=2, tiled=True)
    return lax.psum_scatter(part, "cout", scatter_dimension=0, tiled=True) * factor


def body(volume, first_filter, second_filter, cotangent):
    chans, planes, rows, width = volume.shape
    outs, taps, ins = second_filter.shape
    assert planes == 1 and outs == chans == ins
    plane_count = lax.axis_size("cin")
    row_count = lax.axis_size("cout")
    factor = 1.0 / math.sqrt(plane_count * planes * row_count * rows * width)
    plane_at = lax.axis_index("cin")
    row_at = lax.axis_index("cout")
    where = jnp.stack([plane_at % 2, row_at % 2, row_at // 2, plane_at]).astype(jnp.int32)
    pairwise = plane_count == 4 and row_count == 4
    flops = 2 * 27 * chans * chans * rows * width
    slab = struct((rows, chans, width), BF16)
    field = struct((rows + 2, 3, chans, width), BF16)
    matrix = struct((3 * chans, 9 * chans), BF16)

    stack = struct((3, rows, chans, width), BF16)
    edge = struct((3, chans, width), BF16)

    volume_planes = (swap_planes(volume, 1), swap_planes(volume, 0))
    grad_planes = (swap_planes(cotangent, 1), swap_planes(cotangent, 0))
    first_weights, second_weights, back_weights = call(
        weights_kernel,
        "weights",
        [matrix] * 3,
        (first_filter.transpose(1, 0, 2), second_filter.transpose(1, 0, 2)),
        scalars=False,
    )
    own, across, inside = call(
        gather_kernel,
        "gather_volume",
        [stack, edge, edge],
        (where, volume, after(volume_planes[0], first_weights), volume_planes[1]),
    )
    slabs = (own, swap_rows(inside, 0), swap_rows(across, 1))
    own, across, inside = call(
        gather_kernel,
        "gather_cotangent",
        [stack, edge, edge],
        (where, cotangent, *grad_planes),
    )
    grad_slabs = (own, swap_rows(inside, 0), swap_rows(across, 1))
    hidden, slope, shared = call(
        first_kernel,
        "first_conv",
        [slab, struct(slab.shape, F32), struct((4 * rows + 3, chans, width), BF16)],
        (where, *slabs, first_weights),
        [field],
        flops,
        busy=1,
    )
    pair_shared = swap_rows(shared, 0)
    hidden_odd, hidden_even = swap_planes(hidden, 1), swap_planes(hidden, 0)
    half = struct((rows, chans // 2, width), BF16)
    grads = call(
        grad_kernel,
        "hidden_grad",
        [half, half] if pairwise else [slab],
        (where, *grad_slabs, back_weights, slope),
        [field, struct((chans, width), BF16)],
        flops,
        busy=20,
    )
    shape = (outs // row_count, taps, ins // plane_count)

    def hidden_rows(even, odd):
        own, across, inside = call(
            gather_hidden_kernel, "gather_hidden", [stack, edge, edge], (where, hidden, even, odd)
        )
        return own, swap_rows(inside, 0), swap_rows(across, 1)

    def convolved(*slabs):
        (out,) = call(
            second_kernel,
            "second_conv",
            [struct(volume.shape, BF16)],
            (where, *slabs, second_weights),
            [field, slab],
            flops,
        )
        return out

    if pairwise:
        wide = 2 * rows + 2
        block = shape[0]
        second_send, second_keep = call(
            second_grad_kernel,
            "second_filter_grad",
            [struct((9, block, 3 * ins), BF16), struct((9, block, 3 * ins), F32)],
            (
                where,
                grad_slabs[0],
                swap_rows(grad_slabs[0], 0),
                grad_slabs[2],
                swap_rows(grad_slabs[2], 0),
                hidden,
                pair_shared,
            ),
            [
                struct((wide, 3, 2 * block, width), BF16),
                struct((2 * rows, chans, width), BF16),
                struct((9, 2 * block, 3 * ins), F32),
            ],
            flops,
            busy=0,
        )
        second_arrived = cross(second_send)
        first_send, first_keep = call(
            first_grad_kernel,
            "first_filter_grad",
            [struct((3, block, 9 * ins), BF16), struct((3, block, 9 * ins), F32)],
            (
                where,
                slabs[0],
                slabs[2],
                pair_shared,
                after(grads[0], second_send),
                swap_rows(grads[1], 0),
            ),
            [
                struct((wide, 3, chans, width), BF16),
                struct((2 * rows, 2 * block, width), BF16),
                struct((3, 2 * block, 9 * ins), F32),
            ],
            flops,
            busy=0,
        )
        first_arrived = cross(first_send)
        hidden_slabs = hidden_rows(after(hidden_even, first_send), hidden_odd)
        steps = range(3)
        second_taps = [26 - (a * 9 + b * 3 + e) for b in steps for a in steps for e in steps]
        first_taps = [a * 9 + b * 3 + e for e in steps for b in steps for a in steps]
        *second_parts, second_keep = packed_parts(
            where, after(second_keep, hidden_slabs[1]), second_arrived
        )
        second_parts = exchanged(second_parts)
        *first_parts, first_keep = packed_parts(
            where, after(first_keep, second_keep), first_arrived
        )
        first_parts = exchanged(first_parts)
        second_sum = finished(
            after(second_keep, first_keep), second_parts, second_taps, factor, shape
        )
        second_out = convolved(after(hidden_slabs[0], second_sum), *hidden_slabs[1:])
        first_sum = finished(
            after(first_keep, second_out), first_parts, first_taps, factor, shape
        )
    else:
        second_out = convolved(*hidden_rows(hidden_even, hidden_odd))
        (second_total,) = call(
            second_total_kernel,
            "second_filter_grad",
            [struct((9, outs, 3 * ins), F32)],
            (where, *grad_slabs, hidden),
            [field],
            flops,
        )
        (first_total,) = call(
            first_total_kernel,
            "first_filter_grad",
            [struct((3, outs, 9 * ins), F32)],
            (where, *slabs, *grads),
            [field],
            flops,
        )
        second_total = second_total.reshape(3, 3, outs, 3, ins).transpose(2, 1, 0, 3, 4)
        second_total = jnp.flip(second_total, axis=(1, 2, 3)).reshape(outs, taps, ins)
        first_total = first_total.reshape(3, outs, 3, 3, ins).transpose(1, 3, 2, 0, 4)
        second_sum = scattered(second_total, factor)
        first_sum = scattered(first_total.reshape(outs, taps, ins), factor)
    return (second_out, first_sum, second_sum)


def solution(mesh):
    return jax.shard_map(
        body,
        mesh=mesh,
        in_specs=(
            P(None, ("grp", "cin"), "cout", None),
            P(),
            P(),
            P(None, ("grp", "cin"), "cout", None),
        ),
        out_specs=(
            P(None, ("grp", "cin"), "cout", None),
            P("cout", "grp", "cin"),
            P("cout", "grp", "cin"),
        ),
        check_vma=False,
    )
```

```python
import functools
import math

import jax
import jax.numpy as jnp
from jax import lax
from jax.experimental import pallas as pl
from jax.experimental.pallas import tpu as pltpu
from jax.sharding import PartitionSpec as P

VMEM = pl.BlockSpec(memory_space=pltpu.VMEM)
SMEM = pl.BlockSpec(memory_space=pltpu.SMEM)
F32 = jnp.float32
BF16 = jnp.bfloat16
LIMIT = 14 * 1024 * 1024


def links(count, odd):
    pairs = []
    for i in range(odd, count - 1, 2):
        pairs += [(i, i + 1), (i + 1, i)]
    return pairs


def swap_planes(values, odd):
    return lax.ppermute(values, "cin", links(lax.axis_size("cin"), odd))


def swap_rows(values, odd):
    return lax.ppermute(values, "cout", links(lax.axis_size("cout"), odd))


def shift_up(values):
    lane = lax.broadcasted_iota(jnp.int32, values.shape, 1)
    return jnp.where(lane == 0, 0.0, pltpu.roll(values, 1, 1))


def shift_down(values):
    width = values.shape[1]
    lane = lax.broadcasted_iota(jnp.int32, values.shape, 1)
    return jnp.where(lane == width - 1, 0.0, pltpu.roll(values, width - 1, 1))


def spread(values):
    wide = values.astype(F32)
    return jnp.concatenate(
        [shift_down(wide).astype(BF16), values, shift_up(wide).astype(BF16)], axis=0
    )


def combine(products):
    chans = products.shape[0] // 3
    return (
        products[chans : 2 * chans]
        + shift_up(products[:chans])
        + shift_down(products[2 * chans :])
    )


def planes_of(where):
    return (1, 2 * where[0], 2 * (1 - where[0]))


def fill(where, stack, inside, edges, field):
    rows = field.shape[0] - 2
    row = where[1]
    for plane in range(3):
        for r in range(rows):
            field[1 + r, plane] = stack[plane, r]
        field[(1 - row) * (rows + 1), plane] = inside[plane]
        field[row * (rows + 1), plane] = edges[plane]


def halves(where, quarter):
    mine = where[1]
    return [pl.ds(pl.multiple_of(2 * h * quarter + mine * quarter, quarter), quarter) for h in range(2)]


def fill_pair(where, stack, pair, edges, pair_edges, field, split):
    rows = (field.shape[0] - 2) // 2
    row = where[1]

    def put(at, plane, value):
        if not split:
            field[at, plane] = value[...]
            return
        quarter = field.shape[2] // 2
        for h, part in enumerate(halves(where, quarter)):
            field[at, plane, h * quarter : (h + 1) * quarter] = value[part]

    for plane in range(3):
        for r in range(rows):
            put(1 + row * rows + r, plane, stack.at[plane, r])
            put(1 + (1 - row) * rows + r, plane, pair(plane, r))
        put(row * (2 * rows + 1), plane, edges.at[plane])
        put((1 - row) * (2 * rows + 1), plane, pair_edges.at[plane])


def window(field, row):
    block = field[row : row + 3]
    return block.reshape(-1, block.shape[-1])


def conv_rows(weights, field, row):
    return combine(jnp.dot(weights[...], window(field, row), preferred_element_type=F32))


def gather_kernel(where, own, even, odd, *refs):
    stack, across, inside = refs
    for plane, slab in zip(planes_of(where), (own, odd, even)):
        stack[plane] = jnp.transpose(slab[:, 0], (1, 0, 2))
        across[plane] = stack[plane, where[1] * (stack.shape[1] - 1)]
        inside[plane] = stack[plane, (1 - where[1]) * (stack.shape[1] - 1)]


def hidden_rows_kernel(where, own, even, odd, across, inside):
    last = own.shape[0] - 1
    for plane, slab in zip(planes_of(where), (own, odd, even)):
        across[plane] = slab[where[1] * last]
        inside[plane] = slab[(1 - where[1]) * last]


def weights_kernel(first, second, first_out, second_out, back_out):
    chans = first.shape[1]
    for b in range(3):
        for a in range(3):
            for e in range(3):
                tap = a * 9 + b * 3 + e
                at = (
                    slice(e * chans, (e + 1) * chans),
                    slice((b * 3 + a) * chans, (b * 3 + a + 1) * chans),
                )
                first_out[at] = first[tap]
                second_out[at] = second[tap]
                back_out[at] = second[26 - tap].T


def first_kernel(where, *refs):
    stack, inside, edges, weights, hidden, slope, shared, field = refs
    fill(where, stack, inside, edges, field)
    rows = hidden.shape[0]
    for plane in range(3):
        shared[plane * rows : (plane + 1) * rows] = stack[plane]
    shared[3 * rows : 3 * rows + 3] = edges[...]
    for row in range(hidden.shape[0]):
        value = conv_rows(weights, field, row)
        gate = 1.0 / (1.0 + jnp.exp(-value))
        hidden[row] = (value * gate).astype(BF16)
        shared[3 * rows + 3 + row] = hidden[row]
        slope[row] = gate * (1.0 + value * (1.0 - gate))


def second_kernel(where, own, even, odd, inside, edges, weights, out, field, held):
    rows = held.shape[0]
    row = where[1]
    for plane, slab in zip(planes_of(where), (own, odd, even)):
        for r in range(rows):
            field[1 + r, plane] = slab[r]
    for plane in range(3):
        field[(1 - row) * (rows + 1), plane] = inside[plane]
        field[row * (rows + 1), plane] = edges[plane]
    for at in range(rows):
        held[at] = conv_rows(weights, field, at).astype(BF16)
    out[:, 0] = jnp.transpose(held[...], (1, 0, 2))


def grad_kernel(where, *refs):
    weights, slope, keep, *rest = refs[3:]
    *send, field, whole = rest
    fill(where, *refs[:3], field)
    for row in range(slope.shape[0]):
        grad = (conv_rows(weights, field, row) * slope[row]).astype(BF16)
        if not send:
            keep[row] = grad
        else:
            whole[...] = grad
            quarter = keep.shape[1] // 2
            for h in range(2):
                at = pl.ds(h * quarter, quarter)
                mine = pl.ds(pl.multiple_of((2 * h + where[1]) * quarter, quarter), quarter)
                theirs = pl.ds(pl.multiple_of((2 * h + 1 - where[1]) * quarter, quarter), quarter)
                keep[row, at] = whole[mine]
                send[0][row, at] = whole[theirs]


def pair_off(where, total, send, keep):
    width = send.shape[1]
    mine = pl.multiple_of(where[2] * width, width)
    theirs = pl.multiple_of((1 - where[2]) * width, width)
    send[...] = total[:, pl.ds(theirs, width)].astype(BF16)
    keep[...] = total[:, pl.ds(mine, width)]


def ordered(where, own, pair, both):
    rows = own.shape[0]
    for r in range(rows):
        both[where[1] * rows + r] = own[r]
        both[(1 - where[1]) * rows + r] = pair[r]


def second_grad_kernel(where, *refs):
    stack, pair, edges, pair_edges, hidden, pair_shared, send, keep, field, both, total = refs
    rows = hidden.shape[0]
    fill_pair(where, stack, lambda p, r: pair.at[p, r], edges, pair_edges, field, True)
    ordered(where, hidden, pair_shared.at[pl.ds(3 * rows + 3, rows)], both)
    for row in range(both.shape[0]):
        part = lax.dot_general(
            window(field, row),
            spread(both[row]),
            (((1,), (1,)), ((), ())),
            preferred_element_type=F32,
        ).reshape(total.shape)
        total[...] = part if row == 0 else total[...] + part
    pair_off(where, total, send, keep)


def first_grad_kernel(where, *refs):
    stack, edges, pair_shared, grad, pair_grad, send, keep, field, both, total = refs
    rows = grad.shape[0]
    pair_edges = pair_shared.at[pl.ds(3 * rows, 3)]
    fill_pair(
        where, stack, lambda p, r: pair_shared.at[p * rows + r], edges, pair_edges, field, False
    )
    ordered(where, grad, pair_grad, both)
    for row in range(both.shape[0]):
        part = lax.dot_general(
            spread(both[row]),
            window(field, row),
            (((1,), (1,)), ((), ())),
            preferred_element_type=F32,
        ).reshape(total.shape)
        total[...] = part if row == 0 else total[...] + part
    pair_off(where, total, send, keep)


def second_total_kernel(where, *refs):
    hidden, total, field = refs[3:]
    fill(where, *refs[:3], field)
    for row in range(hidden.shape[0]):
        part = lax.dot_general(
            window(field, row),
            spread(hidden[row]),
            (((1,), (1,)), ((), ())),
            preferred_element_type=F32,
        ).reshape(total.shape)
        total[...] = part if row == 0 else total[...] + part


def first_total_kernel(where, *refs):
    grad, total, field = refs[3:]
    fill(where, *refs[:3], field)
    for row in range(grad.shape[0]):
        part = lax.dot_general(
            spread(grad[row]),
            window(field, row),
            (((1,), (1,)), ((), ())),
            preferred_element_type=F32,
        ).reshape(total.shape)
        total[...] = part if row == 0 else total[...] + part


def pack_kernel(where, held, arrived, *refs):
    sends = refs[:-2]
    keep, packed = refs[-2:]
    parts, tiles, outs, lanes = packed.shape
    group = lanes // parts
    per = held.shape[2] // lanes
    sums = {}
    for n in range(held.shape[0] * per):
        at = (n // per, slice(None), slice(n % per * lanes, (n % per + 1) * lanes))
        sums[n] = held[at] + arrived[at].astype(F32)
    lane = lax.broadcasted_iota(jnp.int32, (outs, lanes), 1) // group
    for tile in range(tiles):
        for part in range(parts):
            value = jnp.zeros((outs, lanes), F32)
            for place in range(parts):
                n = tile * parts + place
                if n in sums:
                    turned = sums[n]
                    if place != part:
                        turned = pltpu.roll(turned, (place - part) % parts * group, 1)
                    value = jnp.where(lane == place, turned, value)
            packed[part, tile] = value
    mine = where[3]
    keep[...] = packed[mine]
    for k, send in enumerate(sends):
        send[...] = packed[mine ^ (k + 1)].astype(BF16)


def finish_kernel(tap_of, factor, held, *refs):
    out = refs[-1]
    tiles, outs, lanes = held.shape
    group = out.shape[2]
    places = lanes // group
    for tile in range(tiles):
        total = held[tile]
        for arrived in refs[:-1]:
            total = total + arrived[tile].astype(F32)
        total = total * factor
        for place in range(places):
            n = tile * places + place
            if n < len(tap_of):
                out[tap_of[n]] = total[:, place * group : (place + 1) * group]


def struct(shape, dtype):
    return jax.ShapeDtypeStruct(shape, dtype)


def call(kernel, name, out_shapes, args, scratch=(), flops=0, scalars=True, busy=1):
    moved = sum(math.prod(a.shape) * a.dtype.itemsize for a in (*args, *out_shapes))
    return pl.pallas_call(
        kernel,
        name=name,
        in_specs=[SMEM] * scalars + [VMEM] * (len(args) - scalars),
        out_specs=[VMEM] * len(out_shapes),
        out_shape=out_shapes,
        scratch_shapes=[pltpu.VMEM(s.shape, s.dtype) for s in scratch],
        cost_estimate=pl.CostEstimate(
            flops=flops * busy, bytes_accessed=moved * busy, transcendentals=0
        ),
        compiler_params=pltpu.CompilerParams(vmem_limit_bytes=LIMIT),
    )(*args)


def after(value, *others):
    return lax.optimization_barrier((value, *others))[0]


def packed_parts(where, keep, arrived):
    taps, outs, width = keep.shape
    parts = lax.axis_size("cin")
    lanes = 128
    tiles = -(-taps * width // (lanes * parts))
    piece = (tiles, outs, lanes)
    return call(
        pack_kernel,
        "pack_parts",
        [struct(piece, BF16)] * (parts - 1) + [struct(piece, F32)],
        (where, keep, arrived),
        [struct((parts, *piece), F32)],
    )


def exchanged(sends):
    parts = lax.axis_size("cin")
    return [
        lax.ppermute(value, "cin", [(i, i ^ (k + 1)) for i in range(parts)])
        for k, value in [(k, sends[k]) for k in (2, 0, 1)]
    ]


def finished(keep, arrived, tap_of, factor, shape):
    (total,) = call(
        functools.partial(finish_kernel, tap_of, factor),
        "finish_sum",
        [struct((shape[1], shape[0], shape[2]), F32)],
        (keep, *arrived),
        scalars=False,
    )
    return total.transpose(1, 0, 2)


def cross(values):
    return lax.ppermute(values, "cout", [(i, i ^ 2) for i in range(lax.axis_size("cout"))])


def scattered(grads, factor):
    part = lax.psum_scatter(grads, "cin", scatter_dimension=2, tiled=True)
    return lax.psum_scatter(part, "cout", scatter_dimension=0, tiled=True) * factor


def body(volume, first_filter, second_filter, cotangent):
    chans, planes, rows, width = volume.shape
    outs, taps, ins = second_filter.shape
    assert planes == 1 and outs == chans == ins
    plane_count = lax.axis_size("cin")
    row_count = lax.axis_size("cout")
    factor = 1.0 / math.sqrt(plane_count * planes * row_count * rows * width)
    plane_at = lax.axis_index("cin")
    row_at = lax.axis_index("cout")
    where = jnp.stack([plane_at % 2, row_at % 2, row_at // 2, plane_at]).astype(jnp.int32)
    pairwise = plane_count == 4 and row_count == 4
    flops = 2 * 27 * chans * chans * rows * width
    slab = struct((rows, chans, width), BF16)
    field = struct((rows + 2, 3, chans, width), BF16)
    matrix = struct((3 * chans, 9 * chans), BF16)

    stack = struct((3, rows, chans, width), BF16)
    edge = struct((3, chans, width), BF16)

    volume_planes = (swap_planes(volume, 0), swap_planes(volume, 1))
    grad_planes = (swap_planes(cotangent, 0), swap_planes(cotangent, 1))
    first_weights, second_weights, back_weights = call(
        weights_kernel,
        "weights",
        [matrix] * 3,
        (first_filter.transpose(1, 0, 2), second_filter.transpose(1, 0, 2)),
        scalars=False,
    )
    own, across, inside = call(
        gather_kernel,
        "gather_volume",
        [stack, edge, edge],
        (where, volume, after(volume_planes[0], first_weights), volume_planes[1]),
    )
    slabs = (own, swap_rows(inside, 0), swap_rows(across, 1))
    own, across, inside = call(
        gather_kernel,
        "gather_cotangent",
        [stack, edge, edge],
        (where, cotangent, *grad_planes),
    )
    grad_slabs = (own, swap_rows(inside, 0), swap_rows(across, 1))
    hidden, slope, shared = call(
        first_kernel,
        "first_conv",
        [slab, struct(slab.shape, F32), struct((4 * rows + 3, chans, width), BF16)],
        (where, *slabs, first_weights),
        [field],
        flops,
        busy=1,
    )
    pair_shared = swap_rows(shared, 0)
    hidden_odd, hidden_even = swap_planes(hidden, 1), swap_planes(hidden, 0)
    half = struct((rows, chans // 2, width), BF16)
    grads = call(
        grad_kernel,
        "hidden_grad",
        [half, half] if pairwise else [slab],
        (where, *grad_slabs, back_weights, slope),
        [field, struct((chans, width), BF16)],
        flops,
        busy=20,
    )
    shape = (outs // row_count, taps, ins // plane_count)

    def hidden_rows(even, odd):
        across, inside = call(
            hidden_rows_kernel, "hidden_rows", [edge, edge], (where, hidden, even, odd)
        )
        return swap_rows(inside, 0), swap_rows(across, 1)

    def convolved(inside, across):
        (out,) = call(
            second_kernel,
            "second_conv",
            [struct(volume.shape, BF16)],
            (where, hidden, hidden_even, hidden_odd, inside, across, second_weights),
            [field, slab],
            flops,
        )
        return out

    if pairwise:
        wide = 2 * rows + 2
        block = shape[0]
        second_send, second_keep = call(
            second_grad_kernel,
            "second_filter_grad",
            [struct((9, block, 3 * ins), BF16), struct((9, block, 3 * ins), F32)],
            (
                where,
                grad_slabs[0],
                swap_rows(grad_slabs[0], 0),
                grad_slabs[2],
                swap_rows(grad_slabs[2], 0),
                hidden,
                pair_shared,
            ),
            [
                struct((wide, 3, 2 * block, width), BF16),
                struct((2 * rows, chans, width), BF16),
                struct((9, 2 * block, 3 * ins), F32),
            ],
            flops,
            busy=0,
        )
        second_arrived = cross(second_send)
        first_send, first_keep = call(
            first_grad_kernel,
            "first_filter_grad",
            [struct((3, block, 9 * ins), BF16), struct((3, block, 9 * ins), F32)],
            (
                where,
                slabs[0],
                slabs[2],
                pair_shared,
                after(grads[0], second_send),
                swap_rows(grads[1], 0),
            ),
            [
                struct((wide, 3, chans, width), BF16),
                struct((2 * rows, 2 * block, width), BF16),
                struct((3, 2 * block, 9 * ins), F32),
            ],
            flops,
            busy=0,
        )
        first_arrived = cross(first_send)
        hidden_edges = hidden_rows(after(hidden_even, first_send), hidden_odd)
        steps = range(3)
        second_taps = [26 - (a * 9 + b * 3 + e) for b in steps for a in steps for e in steps]
        first_taps = [a * 9 + b * 3 + e for e in steps for b in steps for a in steps]
        *second_parts, second_keep = packed_parts(
            where, after(second_keep, hidden_edges[0]), second_arrived
        )
        second_parts = exchanged(second_parts)
        *first_parts, first_keep = packed_parts(
            where, after(first_keep, second_keep), first_arrived
        )
        first_parts = exchanged(first_parts)
        second_sum = finished(
            after(second_keep, first_keep), second_parts, second_taps, factor, shape
        )
        second_out = convolved(after(hidden_edges[0], second_sum), hidden_edges[1])
        first_sum = finished(
            after(first_keep, second_out), first_parts, first_taps, factor, shape
        )
    else:
        second_out = convolved(*hidden_rows(hidden_even, hidden_odd))
        (second_total,) = call(
            second_total_kernel,
            "second_filter_grad",
            [struct((9, outs, 3 * ins), F32)],
            (where, *grad_slabs, hidden),
            [field],
            flops,
        )
        (first_total,) = call(
            first_total_kernel,
            "first_filter_grad",
            [struct((3, outs, 9 * ins), F32)],
            (where, *slabs, *grads),
            [field],
            flops,
        )
        second_total = second_total.reshape(3, 3, outs, 3, ins).transpose(2, 1, 0, 3, 4)
        second_total = jnp.flip(second_total, axis=(1, 2, 3)).reshape(outs, taps, ins)
        first_total = first_total.reshape(3, outs, 3, 3, ins).transpose(1, 3, 2, 0, 4)
        second_sum = scattered(second_total, factor)
        first_sum = scattered(first_total.reshape(outs, taps, ins), factor)
    return (second_out, first_sum, second_sum)


def solution(mesh):
    return jax.shard_map(
        body,
        mesh=mesh,
        in_specs=(
            P(None, ("grp", "cin"), "cout", None),
            P(),
            P(),
            P(None, ("grp", "cin"), "cout", None),
        ),
        out_specs=(
            P(None, ("grp", "cin"), "cout", None),
            P("cout", "grp", "cin"),
            P("cout", "grp", "cin"),
        ),
        check_vma=False,
    )
```
